32 devices in a mesh: query: 4 (over y, x), cand: 2 (over core), tensor: 4 (over z).
Axes of the slice: x: 2, y: 2, z: 4, core: 2. Of those that a mesh axis runs over, the one named last changes fastest.
Arguments:
- cand_states: bfloat16 [8192, 2048], P(('query', 'cand'), 'tensor'), parts along dimension 0, may hold values from -6 to 6
- prefix_states: bfloat16 [256, 2048], P(('query', 'cand'), 'tensor'), parts along dimension 0, may hold values from -6 to 6
- norm_gain: float32 [2048], replicated, may hold values from 0.5 to 1.5
- w_query: bfloat16 [2048, 1024], P(None, 'tensor'), may hold values from -1 to 1
- w_key: bfloat16 [2048, 256], P(None, 'tensor'), may hold values from -1 to 1
- w_value: bfloat16 [2048, 256], P(None, 'tensor'), may hold values from -0.125 to 0.125
- w_out: bfloat16 [1024, 2048], P('tensor'), may hold values from -1.5 to 1.5
- cand_lengths: int32 [64], P(('query', 'cand')), parts along dimension 0, may hold values from 32 to 128, as said below
Outputs:
- attn_out: bfloat16 [8192, 2048], P(('query', 'cand', 'tensor')), parts along dimension 0
The draws below stay inside these ranges and needn't reach their ends.
There are 4 independent parts, one for each index of `query`. The reference program is written for one: setup_inputs(seed, part) draws one part's arguments, and reference() takes and returns one part's arrays. A program takes and returns all parts, laid end to end along the dimension named above; an argument that names none is the same for every part. Nothing has to cross between parts.
Inputs may be any that keep to these rules, and one draw needn't show every extreme that they name: `cand_lengths`: some candidate has all 128 slots live.
All inputs are finite; a program needn't handle non-finite values.
Results may differ from the reference program's by a relative error of at most 0.013.
Values may be sent and summed in bfloat16 or wider, within the bound.
No kernel may reach another device: no remote copies, remote signals or barrier semaphores. Data moves between devices by JAX's collectives and lax.ppermute only.
A program may use at most 64 MiB of HBM per device.

```python
import jax
import jax.numpy as jnp
from jax import lax

D = 2048
HD = 256
PREFIX = 64
CLEN = 128
HEADS = 4
CANDS = 16
ROWS = 2048


def drawn_pair(key):
    shared = jax.random.normal(jax.random.fold_in(key, 11), (D, HD), jnp.float32) * D ** (-0.5)
    spread = jax.random.normal(jax.random.fold_in(key, 12), (D, HEADS * HD), jnp.float32) * D ** (-0.5)
    query_part = spread
    return (jnp.clip(query_part, -1.0, 1.0), jnp.clip(shared, -1.0, 1.0))


def draw_w_query(key, part):
    return drawn_pair(key)[0].astype(jnp.bfloat16)


def draw_w_key(key, part):
    return drawn_pair(key)[1].astype(jnp.bfloat16)


def draw_cand_lengths(key, part):
    lengths = jax.random.randint(jax.random.fold_in(key, 21), (CANDS,), CLEN // 4, CLEN + 1)
    chosen = jax.random.randint(jax.random.fold_in(key, 22), (), 0, CANDS)
    return lengths.at[chosen].set(CLEN).astype(jnp.int32)


def block_scale(stream_key, dims, pieces, low, high):
    def one(axis_at, parts):
        draws = jax.random.uniform(jax.random.fold_in(jax.random.fold_in(stream_key, 6), axis_at), (parts,), jnp.float32, low / len(pieces), high / len(pieces))
        return jnp.repeat(jnp.exp(draws), dims[axis_at] // parts).reshape((-1,) + (1,) * (len(dims) - axis_at - 1))

    loudness = one(*pieces[0])
    for cut in pieces[1:]:
        loudness = loudness * one(*cut)
    return loudness


def scatter_about(own_key, extent, deviation, reach, cuts=(), held_as=jnp.bfloat16):
    level = block_scale(own_key, extent, cuts, -0.22, 0.18) if cuts else 1.0
    values = jax.random.normal(own_key, extent, jnp.float32) * deviation * level
    return jnp.minimum(jnp.maximum(values, -reach), reach).astype(held_as)


def setup_inputs(seed: int = 0, part: int = 0) -> dict:
    arg_keys = jax.random.split(jax.random.key(seed), 9)
    part_keys = jax.random.split(jax.random.fold_in(arg_keys[8], part), 9)
    return {
        "cand_states": scatter_about(part_keys[0], (ROWS, D), 1.0, 6.0, ((0, 2), (1, 4))),
        "prefix_states": scatter_about(part_keys[1], (PREFIX, D), 1.0, 6.0, ((0, 2), (1, 4))),
        "norm_gain": jnp.clip(jax.random.uniform(arg_keys[2], (D,), jnp.float32, 0.5, 1.5), 0.5, 1.5),
        "w_query": draw_w_query(jax.random.fold_in(arg_keys[8], 71), part),
        "w_key": draw_w_key(jax.random.fold_in(arg_keys[8], 71), part),
        "w_value": scatter_about(arg_keys[5], (D, HD), D ** -0.5, 0.125, ((1, 4),)),
        "w_out": scatter_about(arg_keys[6], (HEADS * HD, D), 16 ** -0.5, 1.5, ((0, 4),)),
        "cand_lengths": draw_cand_lengths(jax.random.fold_in(jax.random.fold_in(arg_keys[8], part), 71), part),
    }


epsilon = 1e-06
theta_base = 10000.0

def rotate(values, positions):
    half_size = values.shape[-1] // 2
    frequency = theta_base ** (-jnp.arange(half_size, dtype=jnp.float32) * 2.0 / values.shape[-1])
    angles = positions.astype(jnp.float32)[:, None] * frequency[None, :]
    cosine = jnp.cos(angles)
    sine_part = jnp.sin(angles)
    lower_half = values[:, :half_size]
    upper_half = values[:, half_size:]
    return jnp.concatenate([lower_half * cosine - upper_half * sine_part, upper_half * cosine + lower_half * sine_part], axis=-1)

def normalize(states, norm_gain):
    values = states.astype(jnp.float32)
    square = lax.optimization_barrier(jnp.mean(values * values, axis=-1, keepdims=True))
    return (values * lax.rsqrt(square + epsilon) * norm_gain[None, :]).astype(jnp.bfloat16)

def rounded(values):
    return lax.optimization_barrier(values.astype(jnp.bfloat16)).astype(jnp.float32)

def reference(cand_states, prefix_states, norm_gain, w_query, w_key, w_value, w_out, cand_lengths):
    normed_cand = normalize(cand_states, norm_gain)
    normed_prefix = normalize(prefix_states, norm_gain)
    cand_pos = PREFIX + jnp.tile(jnp.arange(CLEN, dtype=jnp.int32), CANDS)
    prefix_pos = jnp.arange(PREFIX, dtype=jnp.int32)
    cand_keys = rotate(rounded(jnp.dot(normed_cand, w_key, preferred_element_type=jnp.float32)), cand_pos).astype(jnp.bfloat16)
    prefix_keys = rotate(rounded(jnp.dot(normed_prefix, w_key, preferred_element_type=jnp.float32)), prefix_pos).astype(jnp.bfloat16)
    cand_values = jnp.dot(normed_cand, w_value, preferred_element_type=jnp.float32).astype(jnp.bfloat16)
    prefix_values = jnp.dot(normed_prefix, w_value, preferred_element_type=jnp.float32).astype(jnp.bfloat16)
    key_blocks = cand_keys.astype(jnp.float32).reshape(CANDS, CLEN, HD)
    value_blocks = cand_values.astype(jnp.float32).reshape(CANDS, CLEN, HD)
    early_keys = prefix_keys.astype(jnp.float32)
    early_values = prefix_values.astype(jnp.float32)
    slots = jnp.arange(CLEN, dtype=jnp.int32)
    causal = slots[:, None] >= slots[None, :]
    live_rows = slots[None, :] < cand_lengths[:, None]
    summed_out = jnp.zeros((CANDS * CLEN, D), jnp.float32)
    for head_index in range(HEADS):
        query_cols = w_query[:, head_index * HD:(head_index + 1) * HD]
        query_rows = rotate(jnp.dot(normed_cand, query_cols, preferred_element_type=jnp.float32), cand_pos) * HD ** (-0.5)
        queries = rounded(query_rows).reshape(CANDS, CLEN, HD)
        self_scores = jnp.einsum('cqd,ckd->cqk', queries, key_blocks)
        self_scores = jnp.where(causal[None], self_scores, -jnp.inf)
        prefix_scores = jnp.einsum('cqd,kd->cqk', queries, early_keys)
        highest = jnp.maximum(self_scores.max(-1), prefix_scores.max(-1))[..., None]
        self_weights = jnp.exp(self_scores - highest)
        prefix_weights = jnp.exp(prefix_scores - highest)
        divisor = self_weights.sum(-1) + prefix_weights.sum(-1)
        mixture = jnp.einsum('cqk,ckd->cqd', rounded(self_weights), value_blocks)
        mixture = mixture + jnp.einsum('cqk,kd->cqd', rounded(prefix_weights), early_values)
        head_rows = jnp.where(live_rows[..., None], mixture / divisor[..., None], 0.0)
        head_rows = head_rows.reshape(CANDS * CLEN, HD).astype(jnp.bfloat16)
        head_term = jnp.dot(head_rows, w_out[head_index * HD:(head_index + 1) * HD], preferred_element_type=jnp.float32)
        summed_out = summed_out + rounded(head_term)
    return summed_out.astype(jnp.bfloat16)
```

```python
import functools

import jax
import jax.numpy as jnp
from jax import lax
from jax.experimental import pallas as pl
from jax.experimental.pallas import tpu as pltpu
from jax.sharding import PartitionSpec as P


epsilon = 1e-06
theta_base = 10000.0
PLANE = ("query", "cand")


def shift(k):
    n = lax.axis_size("tensor")
    return lambda v: lax.ppermute(v, "tensor", [(i, (i + k) % n) for i in range(n)])


def other_core(v):
    n = lax.axis_size("cand")
    return lax.ppermute(v, "cand", [(i, i ^ 1) for i in range(n)])


def plane_xor(masks):
    nq, nc = lax.axis_size("query"), lax.axis_size("cand")
    pairs = [(q * nc + c, (q ^ masks[c % 2]) * nc + c) for q in range(nq) for c in range(nc)]
    return lambda v: lax.ppermute(v, PLANE, pairs)


def spread(piece):
    bits = lax.axis_size("query").bit_length() - 1
    held = [(piece, (0, 0))]
    for step in range(bits):
        flip = (1 << step, 1 << ((step + 1) % bits))
        held = held + [
            (
                plane_xor(flip)(v),
                (masks[0] ^ flip[0], masks[1] ^ flip[1]),
            )
            for v, masks in held
        ]
    crossed = [(other_core(v), (masks[1], masks[0]), 1) for v, masks in held]
    return [(v, masks, 0) for v, masks in held] + crossed


def rotary_tables(count, half, head_size):
    frequency = theta_base ** (-jnp.arange(half, dtype=jnp.float32) * 2.0 / head_size)
    angles = jnp.arange(count, dtype=jnp.float32)[:, None] * frequency[None, :]
    return jnp.cos(angles), jnp.sin(angles)


def kernel(dims, plan, *refs):
    n, rows, cand_len, prefix_len, depth, head, out_cols = dims
    n_in = 9 + (n - 1) + sum(len(p) for p in plan)
    cand_ref, prefix_ref, gain_ref, cos_ref, sin_ref, len_ref = refs[:6]
    own_q, own_kv, own_out = refs[6:9]
    x_refs = refs[9 : 9 + n - 1]
    piece_refs = refs[9 + n - 1 : n_in]
    o_ref = refs[n_in]
    x_raw, normed, w_in, w_fin, q_scr, kv_scr, heads, sems = refs[n_in + 1 :]
    me = lax.axis_index("tensor")
    q_at = lax.axis_index("query")
    parity = lax.rem(lax.axis_index("cand"), 2)
    width = depth // n
    kv_cols = own_kv.shape[1]
    in_cols = head + kv_cols
    half = head // 2
    share = kv_cols // 2

    count = 0

    def copy(src, dst):
        nonlocal count
        c = pltpu.make_async_copy(src, dst, sems.at[count])
        count += 1
        c.start()
        return c

    def source(k):
        return lax.rem(me - k + n, n)

    x_copies = []
    for k in range(n):
        lanes = pl.ds(pl.multiple_of(source(k) * width, width), width)
        src = cand_ref.at[pl.ds(pl.multiple_of(me * rows, rows), rows), :] if k == 0 else x_refs[k - 1]
        x_copies.append(copy(src, x_raw.at[pl.ds(0, rows), lanes]))
        x_copies.append(copy(prefix_ref.at[k], x_raw.at[pl.ds(rows, prefix_len), lanes]))
    in_copies = [[copy(own_q, w_in.at[0, :, pl.ds(0, head)]), copy(own_kv, w_in.at[0, :, pl.ds(head, kv_cols)])]]
    fin_copies = [[copy(own_out, w_fin.at[0])]]
    at = 0
    where = []
    for k in range(1, n):
        here, later = [], []
        for masks, crossed in plan[k - 1]:
            mask = jnp.where(parity == 0, masks[0], masks[1])
            part = lax.bitwise_xor(q_at, mask) * 2 + (parity if not crossed else 1 - parity)
            ref = piece_refs[at]
            at += 1
            size = ref.shape[0]
            start = pl.multiple_of(part * size, size)
            here.append(copy(ref.at[:, pl.ds(0, in_cols)], w_in.at[k, pl.ds(start, size), :]))
            later.append((ref, start, size))
        in_copies.append(here)
        where.append(later)
    for k in range(1, n):
        fin_copies.append(
            [
                copy(ref.at[:, pl.ds(in_cols, size)], w_fin.at[k, :, pl.ds(start, size)])
                for ref, start, size in where[k - 1]
            ]
        )

    for c in x_copies:
        c.wait()
    block = 32
    gain = gain_ref[...]

    @pl.loop(0, (rows + prefix_len) // block)
    def _(i):
        at_rows = pl.ds(pl.multiple_of(i * block, block), block)
        values = x_raw[at_rows, :].astype(jnp.float32)
        square = jnp.mean(values * values, axis=-1, keepdims=True)
        normed[at_rows, :] = (values * lax.rsqrt(square + epsilon) * gain).astype(jnp.bfloat16)

    cos, sin = cos_ref[...], sin_ref[...]
    cand_cos = jnp.concatenate([cos[prefix_len:]] * (rows // cand_len), axis=0)
    cand_sin = jnp.concatenate([sin[prefix_len:]] * (rows // cand_len), axis=0)

    for k in range(n):
        for c in in_copies[k]:
            c.wait()
        made = jnp.dot(normed[...], w_in[k], preferred_element_type=jnp.float32)
        lower, upper = made[:rows, :half], made[:rows, half:head]
        scale = head ** (-0.5)
        q_scr[k, :, :half] = ((lower * cand_cos - upper * cand_sin) * scale).astype(jnp.bfloat16)
        q_scr[k, :, half:] = ((upper * cand_cos + lower * cand_sin) * scale).astype(jnp.bfloat16)
        kv_scr[source(k)] = made[:, head:].astype(jnp.bfloat16)

    pieces = [kv_scr[s] for s in range(n)]
    low = jnp.concatenate([p[:, :share] for p in pieces[: n // 2]], axis=1).astype(jnp.float32)
    up = jnp.concatenate([p[:, :share] for p in pieces[n // 2 :]], axis=1).astype(jnp.float32)
    all_cos = jnp.concatenate([cand_cos, cos[:prefix_len]], axis=0)
    all_sin = jnp.concatenate([cand_sin, sin[:prefix_len]], axis=0)
    keys = jnp.concatenate(
        [low * all_cos - up * all_sin, up * all_cos + low * all_sin], axis=1
    ).astype(jnp.bfloat16)
    values = jnp.concatenate([p[:, share:] for p in pieces], axis=1)
    prefix_keys, prefix_values = keys[rows:], values[rows:]

    rows_at = lax.broadcasted_iota(jnp.int32, (cand_len, cand_len), 0)
    cols_at = lax.broadcasted_iota(jnp.int32, (cand_len, cand_len), 1)
    causal = rows_at >= cols_at
    slot = lax.broadcasted_iota(jnp.int32, (cand_len, 1), 0)
    trans = (((1,), (1,)), ((), ()))
    for j in range(rows // cand_len):
        own = slice(j * cand_len, (j + 1) * cand_len)
        live = slot < len_ref[me * (rows // cand_len) + j]
        keys_j, values_j = keys[own], values[own]
        for k in range(n):
            queries = q_scr[k, own, :]
            self_s = lax.dot_general(queries, keys_j, trans, preferred_element_type=jnp.float32)
            self_s = jnp.where(causal, self_s, -jnp.inf)
            pre_s = lax.dot_general(queries, prefix_keys, trans, preferred_element_type=jnp.float32)
            top = jnp.maximum(self_s.max(-1, keepdims=True), pre_s.max(-1, keepdims=True))
            self_w = jnp.exp(self_s - top)
            pre_w = jnp.exp(pre_s - top)
            divisor = self_w.sum(-1, keepdims=True) + pre_w.sum(-1, keepdims=True)
            mix = jnp.dot(self_w.astype(jnp.bfloat16), values_j, preferred_element_type=jnp.float32)
            mix = mix + jnp.dot(
                pre_w.astype(jnp.bfloat16), prefix_values, preferred_element_type=jnp.float32
            )
            heads[k, own, :] = jnp.where(live, mix / divisor, 0.0).astype(jnp.bfloat16)

    for group in fin_copies:
        for c in group:
            c.wait()
    tile = min(512, out_cols)
    for col in range(0, out_cols, tile):
        total = None
        for k in range(n):
            term = jnp.dot(
                heads[k], w_fin[k, :, col : col + tile], preferred_element_type=jnp.float32
            )
            term = term.astype(jnp.bfloat16).astype(jnp.float32)
            total = term if total is None else total + term
        o_ref[:, col : col + tile] = total.astype(jnp.bfloat16)


def body(cand_states, prefix_states, norm_gain, w_query, w_key, w_value, w_out, cand_lengths):
    n = lax.axis_size("tensor")
    nq, nc = lax.axis_size("query"), lax.axis_size("cand")
    me = lax.axis_index("tensor")
    part = lax.axis_index("query") * 2 + lax.axis_index("cand") % 2
    depth, head = w_query.shape
    out_cols = w_out.shape[1]
    size = depth // (2 * nq)
    cand_len = cand_states.shape[0] // cand_lengths.shape[0]
    rows = cand_states.shape[0] // n
    prefix_len = prefix_states.shape[0] * nc
    half = head // 2

    def take(v, at, size, axis):
        return lax.dynamic_slice_in_dim(v, at * size, size, axis)

    own_kv = jnp.concatenate([w_key, w_value], axis=1)
    piece = jnp.concatenate(
        [
            take(w_query, part, size, 0),
            take(w_key, part, size, 0),
            take(w_value, part, size, 0),
            take(w_out, part, size, 1),
        ],
        axis=1,
    )
    moved = {1: shift(1)(piece)}
    if n > 2:
        moved[n - 1] = shift(n - 1)(piece)
    for k in range(2, n - 1):
        moved[k] = shift(1)(moved[k - 1])
    pre = [prefix_states] + [shift(k)(prefix_states) for k in range(1, n)]
    xs = [shift(k)(take(cand_states, (me + k) % n, rows, 0)) for k in range(1, n)]
    pre = jnp.stack(pre)
    if nc == 2:
        far = other_core(pre)
        even = lax.axis_index("cand") == 0
        pre = jnp.where(
            even, jnp.concatenate([pre, far], axis=1), jnp.concatenate([far, pre], axis=1)
        )
    else:
        pre = lax.all_gather(pre, "cand", axis=1, tiled=True)
    spreads = [spread(moved[k]) for k in range(1, n)]
    plan = tuple(tuple((masks, crossed) for _, masks, crossed in s) for s in spreads)
    pieces = [v for s in spreads for v, _, _ in s]
    cos, sin = rotary_tables(prefix_len + cand_len, half, head)

    dims = (n, rows, cand_len, prefix_len, depth, head, out_cols)
    any_spec = pl.BlockSpec(memory_space=pl.ANY)
    vmem = pl.BlockSpec(memory_space=pltpu.VMEM)
    smem = pl.BlockSpec(memory_space=pltpu.SMEM)
    kv_cols = own_kv.shape[1]
    return pl.pallas_call(
        functools.partial(kernel, dims, plan),
        name="main",
        out_shape=jax.ShapeDtypeStruct((rows, out_cols), jnp.bfloat16),
        in_specs=[any_spec, any_spec, vmem, vmem, vmem, smem]
        + [any_spec] * (3 + len(xs) + len(pieces)),
        out_specs=vmem,
        scratch_shapes=[
            pltpu.VMEM((rows + prefix_len, depth), jnp.bfloat16),
            pltpu.VMEM((rows + prefix_len, depth), jnp.bfloat16),
            pltpu.VMEM((n, depth, head + kv_cols), jnp.bfloat16),
            pltpu.VMEM((n, head, out_cols), jnp.bfloat16),
            pltpu.VMEM((n, rows, head), jnp.bfloat16),
            pltpu.VMEM((n, rows + prefix_len, kv_cols), jnp.bfloat16),
            pltpu.VMEM((n, rows, head), jnp.bfloat16),
            pltpu.SemaphoreType.DMA((2 * n + 3 + 2 * len(pieces),)),
        ],
        compiler_params=pltpu.CompilerParams(vmem_limit_bytes=40 * 2**20),
    )(
        cand_states, pre, norm_gain.reshape(1, depth), cos, sin, cand_lengths,
        w_query, own_kv, w_out, *xs, *pieces,
    )


def solution(mesh):
    in_specs = (
        P(("query", "cand"), "tensor"),
        P(("query", "cand"), "tensor"),
        P(),
        P(None, "tensor"),
        P(None, "tensor"),
        P(None, "tensor"),
        P("tensor", None),
        P(("query", "cand")),
    )
    out_specs = P(("query", "cand", "tensor"), None)

    return jax.shard_map(body, mesh=mesh, in_specs=in_specs, out_specs=out_specs, check_vma=False)
```

```python
import functools

import jax
import jax.numpy as jnp
from jax import lax
from jax.experimental import pallas as pl
from jax.experimental.pallas import tpu as pltpu
from jax.sharding import PartitionSpec as P


epsilon = 1e-06
theta_base = 10000.0
PLANE = ("query", "cand")


def shift(k):
    n = lax.axis_size("tensor")
    return lambda v: lax.ppermute(v, "tensor", [(i, (i + k) % n) for i in range(n)])


def other_core(v):
    n = lax.axis_size("cand")
    return lax.ppermute(v, "cand", [(i, i ^ 1) for i in range(n)])


def plane_xor(masks):
    nq, nc = lax.axis_size("query"), lax.axis_size("cand")
    pairs = [(q * nc + c, (q ^ masks[c % 2]) * nc + c) for q in range(nq) for c in range(nc)]
    return lambda v: lax.ppermute(v, PLANE, pairs)


def spread(whole, piece):
    bits = lax.axis_size("query").bit_length() - 1
    held = [(piece, (0, 0))]
    for step in range(bits):
        flip = (1 << step, 1 << ((step + 1) % bits))
        held = held + [
            (
                plane_xor(flip)(v),
                (masks[0] ^ flip[0], masks[1] ^ flip[1]),
            )
            for v, masks in held
        ]
    held[0] = (whole, held[0][1])
    crossed = [(other_core(v), (masks[1], masks[0]), 1) for v, masks in held]
    return [(v, masks, 0) for v, masks in held] + crossed


def nearest(n):
    hops = [1] + [n - 1] * (n > 2) + list(range(2, n - 1))
    return [tuple((t - k) % n for t in range(n)) for k in hops]


def pick_kernel(choice, count, *refs):
    in_refs, o_refs = refs[:count], refs[count:]
    me = lax.axis_index("tensor")
    for i, ref in enumerate(in_refs):
        wanted = functools.reduce(
            jnp.logical_or, [me == t for t, which in enumerate(choice) if which == i]
        )

        @pl.when(wanted)
        def _(ref=ref):
            for o in o_refs:
                o[...] = ref[: o.shape[0], :]


def pick(by_place, heights, whole=None):
    distinct = []
    for v in by_place:
        if not any(v is d for d in distinct):
            distinct.append(v)
    choice = [next(i for i, d in enumerate(distinct) if d is v) for v in by_place]
    width = distinct[0].shape[1]
    made = pl.pallas_call(
        functools.partial(pick_kernel, choice, len(distinct)),
        out_shape=[jax.ShapeDtypeStruct((h, width), distinct[0].dtype) for h in heights],
        in_specs=[pl.BlockSpec(memory_space=pltpu.VMEM)] * len(distinct),
        out_specs=[pl.BlockSpec(memory_space=pltpu.VMEM)] * len(heights),
        compiler_params=pltpu.CompilerParams(vmem_limit_bytes=4 * 2**20),
    )(*distinct)
    return made if whole is None else [whole] + list(made)


def along_line(piece, height):
    n = lax.axis_size("tensor")
    came = {1: shift(1)(piece)}
    if n > 2:
        came[n - 1] = shift(n - 1)(piece)
    for k in range(2, n - 1):
        came[k] = shift(1)(came[k - 1])
    hops = [1] + [n - 1] * (n > 2) + list(range(2, n - 1))
    return [pick([came[k]] * n, (height,), came[k]) for k in hops]


def prefix_blocks(row, parity, prefix_rows, prefix_len, width, size):
    if 2 * prefix_rows == prefix_len:
        return [
            (row + i * prefix_rows, prefix_rows, parity * prefix_rows, i * size)
            for i in range(width // size)
        ]
    return [(row, prefix_len, 0, parity * size)]


def cut_kernel(dims, q_ref, out_ref, k_ref, v_ref, p_ref, o_ref, sems):
    prefix_rows, prefix_len, width = dims
    size, head = o_ref.shape[1], out_ref.shape[0]
    share = k_ref.shape[0]
    parity = lax.rem(lax.axis_index("cand"), 2)
    part = (lax.axis_index("query") * 2 + parity) * size
    at = pl.ds(pl.multiple_of(part, size), size)
    copies = []

    def copy(src, row, count):
        copies.append(
            pltpu.make_async_copy(src, o_ref.at[pl.ds(row, count), :], sems.at[len(copies)])
        )

    half, half_head = size // 2, head // 2
    for i in range(2):
        copy(q_ref.at[pl.ds(pl.multiple_of(part + i * half, half), half), :], i * half, half)
        copy(out_ref.at[pl.ds(i * half_head, half_head), at], size + i * half_head, half_head)
    copy(k_ref.at[:, at], size + head, share)
    copy(v_ref.at[:, at], size + head + share, share)
    blocks = prefix_blocks(size + head + 2 * share, parity, prefix_rows, prefix_len, width, size)
    for row, count, start, lane in blocks:
        if 2 * prefix_rows == prefix_len:
            start = 0
        lanes = pl.ds(pl.multiple_of(lane, size), size)
        copy(p_ref.at[pl.ds(start, count), lanes], row, count)
    for c in copies:
        c.start()
    for c in copies:
        c.wait()


def rotary_tables(count, half, head_size):
    frequency = theta_base ** (-jnp.arange(half, dtype=jnp.float32) * 2.0 / head_size)
    angles = jnp.arange(count, dtype=jnp.float32)[:, None] * frequency[None, :]
    return jnp.cos(angles), jnp.sin(angles)


def kernel(dims, rounds, plan, *refs):
    n, rows, cand_len, prefix_rows, prefix_len, depth, head, _ = dims
    n_pieces = len(plan)
    n_in = 11 + (n - 1) + (n - 1) * n_pieces
    cand_ref, gain_ref, cos_ref, sin_ref, len_ref = refs[:5]
    prefix_refs = refs[5:7]
    own_q, own_out, own_k, own_v = refs[7:11]
    x_refs = refs[11 : 11 + n - 1]
    piece_refs = refs[11 + n - 1 : n_in]
    o_ref = refs[n_in]
    x_own, w_query, w_out, w_kv, p_raw, normed, kv_scr, q_scr, heads, sems = refs[n_in + 1 :]
    me = lax.axis_index("tensor")
    q_at = lax.axis_index("query")
    parity = lax.rem(lax.axis_index("cand"), 2)
    width = depth // n
    half = head // 2
    share = own_k.shape[0]
    size = w_query.shape[1]
    chunks = width // size

    def rows_of(start, size):
        return pl.ds(pl.multiple_of(start, size), size)

    def table(places):
        value = places[0]
        for t in range(1, n):
            value = jnp.where(me == t, places[t], value)
        return value

    moves = [
        (cand_ref.at[rows_of(me * rows, rows), :], x_own),
        (own_k, w_kv.at[pl.ds(0, share), :]),
        (own_v, w_kv.at[pl.ds(share, share), :]),
        (own_q, w_query),
        (own_out, w_out),
    ]
    copies = [pltpu.make_async_copy(src, dst, sems.at[i]) for i, (src, dst) in enumerate(moves)]
    for c in copies:
        c.start()

    sources = [me] + [table(places) for places in rounds]
    pieces = [piece_refs[r * n_pieces : (r + 1) * n_pieces] for r in range(n - 1)]
    parts = []
    for masks, crossed in plan:
        mask = jnp.where(parity == 0, masks[0], masks[1])
        parts.append(lax.bitwise_xor(q_at, mask) * 2 + (parity if not crossed else 1 - parity))

    fixed = size + head + 2 * share
    prefix_in = [prefix_refs] + [(p[0], p[n_pieces // 2]) for p in pieces]
    for source, both in zip(sources, prefix_in):
        for ref, side in zip(both, (parity, 1 - parity)):
            for at, count, start, lane in prefix_blocks(
                fixed, side, prefix_rows, prefix_len, width, size
            ):
                to = rows_of(start, count) if 2 * prefix_rows == prefix_len else pl.ds(start, count)
                p_raw[source * chunks + lane // size, to, :] = ref[pl.ds(at, count), :]

    block = 32

    def normalise(parts_in, to_rows):
        values = [v.astype(jnp.float32) for _, v in parts_in]
        square = sum(jnp.sum(v * v, axis=-1, keepdims=True) for v in values) / depth
        scale = lax.rsqrt(square + epsilon)
        for (chunk, _), v in zip(parts_in, values):
            normed[chunk, to_rows, :] = (v * scale * gain_ref[chunk]).astype(jnp.bfloat16)

    @pl.loop(0, prefix_len // block)
    def _(i):
        at = rows_of(i * block, block)
        to = pl.ds(pl.multiple_of(rows + i * block, block), block)
        normalise([(c, p_raw[c, at, :]) for c in range(n * chunks)], to)

    copies[0].wait()
    x_all = [x_own] + list(x_refs)
    x_from = [me] + [lax.rem(me - k + n, n) for k in range(1, n)]

    @pl.loop(0, rows // block)
    def _(i):
        at = rows_of(i * block, block)
        normalise(
            [
                (source * chunks + h, ref[at, pl.ds(h * size, size)])
                for source, ref in zip(x_from, x_all)
                for h in range(chunks)
            ],
            at,
        )

    cos, sin = cos_ref[...], sin_ref[...]
    cand_cos = jnp.concatenate([cos[prefix_len:]] * (rows // cand_len), axis=0)
    cand_sin = jnp.concatenate([sin[prefix_len:]] * (rows // cand_len), axis=0)
    all_cos = jnp.concatenate([cand_cos, cos[:prefix_len]], axis=0)
    all_sin = jnp.concatenate([cand_sin, sin[:prefix_len]], axis=0)
    trans = (((1,), (1,)), ((), ()))

    copies[1].wait()
    copies[2].wait()
    made = None
    for i, part in enumerate(parts):
        weights = jnp.concatenate(
            [w_kv[:, rows_of(part * size, size)]]
            + [p[i][pl.ds(size + head, 2 * share), :] for p in pieces],
            axis=0,
        )
        term = lax.dot_general(normed[part], weights, trans, preferred_element_type=jnp.float32)
        made = term if made is None else made + term
    for k, source in enumerate(sources):
        kv_scr[source] = made[:, k * 2 * share : (k + 1) * 2 * share].astype(jnp.bfloat16)
    shares = [kv_scr[s] for s in range(n)]
    low = jnp.concatenate([p[:, :share] for p in shares[: n // 2]], axis=1).astype(jnp.float32)
    up = jnp.concatenate([p[:, :share] for p in shares[n // 2 :]], axis=1).astype(jnp.float32)
    keys = jnp.concatenate(
        [low * all_cos - up * all_sin, up * all_cos + low * all_sin], axis=1
    ).astype(jnp.bfloat16)
    values = jnp.concatenate([p[:, share:] for p in shares], axis=1)
    prefix_keys, prefix_values = keys[rows:], values[rows:]

    scale = head ** (-0.5)
    for k in range(n - 1, -1, -1):
        if k == 0:
            copies[3].wait()
        made = None
        for i, part in enumerate(parts):
            if k == 0:
                weights = w_query[rows_of(part * size, size), :]
            else:
                weights = pieces[k - 1][i][pl.ds(0, size), :]
            term = jnp.dot(
                normed[part, pl.ds(0, rows), :], weights, preferred_element_type=jnp.float32
            )
            made = term if made is None else made + term
        lower, upper = made[:, :half], made[:, half:]
        q_scr[k, :, :half] = ((lower * cand_cos - upper * cand_sin) * scale).astype(jnp.bfloat16)
        q_scr[k, :, half:] = ((upper * cand_cos + lower * cand_sin) * scale).astype(jnp.bfloat16)

    tall = (n, cand_len, cand_len + prefix_len)
    slot = lax.broadcasted_iota(jnp.int32, tall, 1).reshape(n * cand_len, tall[2])
    other = lax.broadcasted_iota(jnp.int32, tall, 2).reshape(n * cand_len, tall[2])
    seen = (slot >= other) | (other >= cand_len)
    for j in range(rows // cand_len):
        own = slice(j * cand_len, (j + 1) * cand_len)
        live = slot[:, :1] < len_ref[me * (rows // cand_len) + j]
        keys_j = jnp.concatenate([keys[own], prefix_keys], axis=0)
        values_j = jnp.concatenate([values[own], prefix_values], axis=0)
        queries = jnp.concatenate([q_scr[k, own, :] for k in range(n)], axis=0)
        scores = lax.dot_general(queries, keys_j, trans, preferred_element_type=jnp.float32)
        scores = jnp.where(seen, scores, -jnp.inf)
        weights = jnp.exp(scores - scores.max(-1, keepdims=True))
        divisor = weights.sum(-1, keepdims=True)
        mix = jnp.dot(weights.astype(jnp.bfloat16), values_j, preferred_element_type=jnp.float32)
        mix = jnp.where(live, mix / divisor, 0.0).astype(jnp.bfloat16)
        for k in range(n):
            heads[k, own, :] = mix[k * cand_len : (k + 1) * cand_len]

    copies[4].wait()
    for i, part in enumerate(parts):
        spot = rows_of(part * size, size)
        total = None
        for k in range(n):
            weights = w_out[:, spot] if k == 0 else pieces[k - 1][i][pl.ds(size, head), :]
            term = jnp.dot(heads[k], weights, preferred_element_type=jnp.float32)
            term = term.astype(jnp.bfloat16).astype(jnp.float32)
            total = term if total is None else total + term
        o_ref[:, spot] = total.astype(jnp.bfloat16)


def body(cand_states, prefix_states, norm_gain, w_query, w_key, w_value, w_out, cand_lengths):
    n = lax.axis_size("tensor")
    nq, nc = lax.axis_size("query"), lax.axis_size("cand")
    me = lax.axis_index("tensor")
    depth, head = w_query.shape
    share = w_key.shape[1]
    out_cols = w_out.shape[1]
    size = depth // (2 * nq)
    cand_len = cand_states.shape[0] // cand_lengths.shape[0]
    rows = cand_states.shape[0] // n
    prefix_len = prefix_states.shape[0] * nc
    half = head // 2
    any_spec = pl.BlockSpec(memory_space=pl.ANY)
    hbm = pl.BlockSpec(memory_space=pltpu.HBM)
    vmem = pl.BlockSpec(memory_space=pltpu.VMEM)
    smem = pl.BlockSpec(memory_space=pltpu.SMEM)

    key_t, value_t = w_key.T, w_value.T
    prefix_rows = prefix_states.shape[0]
    near = prefix_states
    if 2 * prefix_rows != prefix_len:
        near = lax.all_gather(prefix_states, "cand", axis=0, tiled=True)
    height = size + head + 2 * share
    tail = prefix_rows * (cand_states.shape[1] // size) if near is prefix_states else prefix_len
    piece = pl.pallas_call(
        functools.partial(cut_kernel, (prefix_rows, prefix_len, cand_states.shape[1])),
        name="cut",
        out_shape=jax.ShapeDtypeStruct((height + tail, size), jnp.bfloat16),
        in_specs=[any_spec] * 5,
        out_specs=vmem,
        scratch_shapes=[pltpu.SemaphoreType.DMA((8,))],
        compiler_params=pltpu.CompilerParams(vmem_limit_bytes=60 * 2**20),
    )(w_query, w_out, key_t, value_t, near)
    moved = along_line(piece, height)
    xs = [
        shift(k)(lax.dynamic_slice_in_dim(cand_states, (me + k) % n * rows, rows, 0))
        for k in range(1, n)
    ]
    across = other_core(piece)
    spreads = [spread(whole, v) for whole, v in moved]
    plan = tuple((masks, crossed) for _, masks, crossed in spreads[0])
    pieces = [v for s in spreads for v, _, _ in s]
    cos, sin = rotary_tables(prefix_len + cand_len, half, head)

    dims = (n, rows, cand_len, prefix_rows, prefix_len, depth, head, out_cols)
    return pl.pallas_call(
        functools.partial(kernel, dims, nearest(n), plan),
        name="main",
        out_shape=jax.ShapeDtypeStruct((rows, out_cols), jnp.bfloat16),
        in_specs=[hbm, vmem, vmem, vmem, smem]
        + [vmem] * 2
        + [hbm] * 4
        + [vmem] * (len(xs) + len(pieces)),
        out_specs=vmem,
        scratch_shapes=[
            pltpu.VMEM((rows, depth // n), jnp.bfloat16),
            pltpu.VMEM((depth, head), jnp.bfloat16),
            pltpu.VMEM((head, out_cols), jnp.bfloat16),
            pltpu.VMEM((2 * share, depth), jnp.bfloat16),
            pltpu.VMEM((depth // size, prefix_len, size), jnp.bfloat16),
            pltpu.VMEM((depth // size, rows + prefix_len, size), jnp.bfloat16),
            pltpu.VMEM((n, rows + prefix_len, 2 * share), jnp.bfloat16),
            pltpu.VMEM((n, rows, head), jnp.bfloat16),
            pltpu.VMEM((n, rows, head), jnp.bfloat16),
            pltpu.SemaphoreType.DMA((5,)),
        ],
        compiler_params=pltpu.CompilerParams(vmem_limit_bytes=32 * 2**20),
    )(
        cand_states, norm_gain.reshape(depth // size, 1, size), cos, sin, cand_lengths,
        piece, across, w_query, w_out, key_t, value_t, *xs, *pieces,
    )


def solution(mesh):
    in_specs = (
        P(("query", "cand"), "tensor"),
        P(("query", "cand"), "tensor"),
        P(),
        P(None, "tensor"),
        P(None, "tensor"),
        P(None, "tensor"),
        P("tensor", None),
        P(("query", "cand")),
    )
    out_specs = P(("query", "cand", "tensor"), None)

    return jax.shard_map(body, mesh=mesh, in_specs=in_specs, out_specs=out_specs, check_vma=False)
```

```python
import functools

import jax
import jax.numpy as jnp
from jax import lax
from jax.experimental import pallas as pl
from jax.experimental.pallas import tpu as pltpu
from jax.sharding import PartitionSpec as P


epsilon = 1e-06
theta_base = 10000.0
PLANE = ("query", "cand")
UNROLL = 4


def shift(k):
    n = lax.axis_size("tensor")
    return lambda v: lax.ppermute(v, "tensor", [(i, (i + k) % n) for i in range(n)])


def other_core(v):
    n = lax.axis_size("cand")
    return lax.ppermute(v, "cand", [(i, i ^ 1) for i in range(n)])


def plane_xor(masks):
    nq, nc = lax.axis_size("query"), lax.axis_size("cand")
    pairs = [(q * nc + c, (q ^ masks[c % 2]) * nc + c) for q in range(nq) for c in range(nc)]
    return lambda v: lax.ppermute(v, PLANE, pairs)


def spread(whole, piece):
    bits = lax.axis_size("query").bit_length() - 1
    held = [(piece, (0, 0))]
    for step in range(bits):
        flip = (1 << step, 1 << ((step + 1) % bits))
        held = held + [
            (
                plane_xor(flip)(v),
                (masks[0] ^ flip[0], masks[1] ^ flip[1]),
            )
            for v, masks in held
        ]
    held[0] = (whole, held[0][1])
    crossed = [(other_core(v), (masks[1], masks[0]), 1) for v, masks in held]
    return [(v, masks, 0) for v, masks in held] + crossed


def nearest(n):
    hops = [1] + [n - 1] * (n > 2) + list(range(2, n - 1))
    return [tuple((t - k) % n for t in range(n)) for k in hops]


def pick_kernel(choice, count, *refs):
    in_refs, o_refs = refs[:count], refs[count:]
    me = lax.axis_index("tensor")
    for i, ref in enumerate(in_refs):
        wanted = functools.reduce(
            jnp.logical_or, [me == t for t, which in enumerate(choice) if which == i]
        )

        @pl.when(wanted)
        def _(ref=ref):
            for o in o_refs:
                o[...] = ref[: o.shape[0], :]


def pick(by_place, heights, whole=None):
    distinct = []
    for v in by_place:
        if not any(v is d for d in distinct):
            distinct.append(v)
    choice = [next(i for i, d in enumerate(distinct) if d is v) for v in by_place]
    width = distinct[0].shape[1]
    made = pl.pallas_call(
        functools.partial(pick_kernel, choice, len(distinct)),
        out_shape=[jax.ShapeDtypeStruct((h, width), distinct[0].dtype) for h in heights],
        in_specs=[pl.BlockSpec(memory_space=pltpu.VMEM)] * len(distinct),
        out_specs=[pl.BlockSpec(memory_space=pltpu.VMEM)] * len(heights),
        compiler_params=pltpu.CompilerParams(vmem_limit_bytes=4 * 2**20),
    )(*distinct)
    return made if whole is None else [whole] + list(made)


def along_line(piece, height):
    n = lax.axis_size("tensor")
    came = {1: shift(1)(piece)}
    if n > 2:
        came[n - 1] = shift(n - 1)(piece)
    for k in range(2, n - 1):
        came[k] = shift(1)(came[k - 1])
    hops = [1] + [n - 1] * (n > 2) + list(range(2, n - 1))
    return [pick([came[k]] * n, (height,), came[k]) for k in hops]


def prefix_blocks(row, parity, prefix_rows, prefix_len, width, size):
    if 2 * prefix_rows == prefix_len:
        return [
            (row + i * prefix_rows, prefix_rows, parity * prefix_rows, i * size)
            for i in range(width // size)
        ]
    return [(row, prefix_len, 0, parity * size)]


def cut_kernel(dims, q_ref, out_ref, k_ref, v_ref, p_ref, o_ref, sems):
    prefix_rows, prefix_len, width = dims
    size, head = o_ref.shape[1], out_ref.shape[0]
    share = k_ref.shape[0]
    parity = lax.rem(lax.axis_index("cand"), 2)
    part = (lax.axis_index("query") * 2 + parity) * size
    at = pl.ds(pl.multiple_of(part, size), size)
    copies = []

    def copy(src, row, count):
        copies.append(
            pltpu.make_async_copy(src, o_ref.at[pl.ds(row, count), :], sems.at[len(copies)])
        )

    half, half_head = size // 2, head // 2
    for i in range(2):
        copy(q_ref.at[pl.ds(pl.multiple_of(part + i * half, half), half), :], i * half, half)
        copy(out_ref.at[pl.ds(i * half_head, half_head), at], size + i * half_head, half_head)
    copy(k_ref.at[:, at], size + head, share)
    copy(v_ref.at[:, at], size + head + share, share)
    blocks = prefix_blocks(size + head + 2 * share, parity, prefix_rows, prefix_len, width, size)
    for row, count, start, lane in blocks:
        if 2 * prefix_rows == prefix_len:
            start = 0
        lanes = pl.ds(pl.multiple_of(lane, size), size)
        copy(p_ref.at[pl.ds(start, count), lanes], row, count)
    for c in copies:
        c.start()
    for c in copies:
        c.wait()


def rotary_tables(count, half, head_size):
    frequency = theta_base ** (-jnp.arange(half, dtype=jnp.float32) * 2.0 / head_size)
    angles = jnp.arange(count, dtype=jnp.float32)[:, None] * frequency[None, :]
    return jnp.cos(angles), jnp.sin(angles)


def rows_of(start, size):
    return pl.ds(pl.multiple_of(start, size), size)


def places(rounds, plan, q_at, me, parity):
    sources = []
    for by_place in rounds:
        value = by_place[0]
        for t in range(1, len(by_place)):
            value = jnp.where(me == t, by_place[t], value)
        sources.append(value)
    parts = []
    for masks, crossed in plan:
        mask = jnp.where(parity == 0, masks[0], masks[1])
        parts.append(lax.bitwise_xor(q_at, mask) * 2 + (parity if not crossed else 1 - parity))
    return sources, parts


def add_up(terms):
    chains = [functools.reduce(jnp.add, terms[i::2]) for i in range(2)]
    return chains[0] + chains[1]


def rotated(lower, upper, cos, sin):
    return lower * cos - upper * sin, upper * cos + lower * sin


TRANS = (((1,), (1,)), ((), ()))


def first_kernel(dims, rounds, plan, *refs):
    n, rows, cand_len, prefix_rows, prefix_len, depth, head, _ = dims
    n_pieces = len(plan)
    count = n - 2
    cand_ref, gain_ref, cos_ref, sin_ref = refs[:4]
    prefix_refs = refs[4:8]
    own_q, own_k, own_v = refs[8:11]
    x_refs = refs[11 : 11 + n - 1]
    n_in = 11 + n - 1 + count * n_pieces
    piece_refs = refs[11 + n - 1 : n_in]
    normed, q_ref, kv_ref = refs[n_in : n_in + 3]
    x_own, w_query, w_kv, p_raw, sems = refs[n_in + 3 :]
    me = lax.axis_index("tensor")
    parity = lax.rem(lax.axis_index("cand"), 2)
    width = depth // n
    half = head // 2
    share = own_k.shape[0]
    size = w_query.shape[1]
    chunks = width // size

    moves = [
        (cand_ref.at[rows_of(me * rows, rows), :], x_own),
        (own_k, w_kv.at[pl.ds(0, share), :]),
        (own_v, w_kv.at[pl.ds(share, share), :]),
        (own_q, w_query),
    ]
    copies = [pltpu.make_async_copy(src, dst, sems.at[i]) for i, (src, dst) in enumerate(moves)]
    for c in copies:
        c.start()
    sources, parts = places(rounds, plan, lax.axis_index("query"), me, parity)
    sources = [me] + sources
    pieces = [piece_refs[r * n_pieces : (r + 1) * n_pieces] for r in range(count)]

    fixed = size + head + 2 * share
    prefix_in = [prefix_refs[:2]] + [(p[0], p[n_pieces // 2]) for p in pieces] + [prefix_refs[2:]]
    for source, both in zip(sources, prefix_in):
        for ref, side in zip(both, (parity, 1 - parity)):
            for at, height, start, lane in prefix_blocks(
                fixed, side, prefix_rows, prefix_len, width, size
            ):
                whole = 2 * prefix_rows != prefix_len
                to = pl.ds(start, height) if whole else rows_of(start, height)
                p_raw[source * chunks + lane // size, to, :] = ref[pl.ds(at, height), :]

    block = 32

    def normalise(parts_in, to_rows):
        values = [ref[at].astype(jnp.float32) for _, ref, at in parts_in]
        square = sum(v * v for v in values)
        square = jnp.sum(square, axis=-1, keepdims=True) / depth
        scale = lax.rsqrt(square + epsilon)
        for (chunk, ref, at), v in zip(parts_in, values):
            normed[chunk, to_rows, :] = (v * scale * gain_ref[chunk]).astype(jnp.bfloat16)

    def prefix_block(i, carry):
        at = rows_of(i * block, block)
        to = pl.ds(pl.multiple_of(rows + i * block, block), block)
        normalise([(c, p_raw, (c, at, slice(None))) for c in range(n * chunks)], to)
        return carry

    lax.fori_loop(0, prefix_len // block, prefix_block, 0, unroll=UNROLL)
    copies[0].wait()
    x_from = [me] + [lax.rem(me - k + n, n) for k in range(1, n)]

    def cand_block(i, carry):
        at = rows_of(i * block, block)
        normalise(
            [
                (source * chunks + h, ref, (at, pl.ds(h * size, size)))
                for source, ref in zip(x_from, [x_own] + list(x_refs))
                for h in range(chunks)
            ],
            at,
        )
        return carry

    lax.fori_loop(0, rows // block, cand_block, 0, unroll=UNROLL)

    for c in copies[1:3]:
        c.wait()
    made = []
    for i, part in enumerate(parts):
        weights = jnp.concatenate(
            [w_kv[:, rows_of(part * size, size)]]
            + [p[i][pl.ds(size + head, 2 * share), :] for p in pieces],
            axis=0,
        )
        made.append(
            lax.dot_general(normed[part], weights, TRANS, preferred_element_type=jnp.float32)
        )
    made = functools.reduce(jnp.add, made).astype(jnp.bfloat16)
    for k in range(n - 1):
        kv_ref[k] = made[:, k * 2 * share : (k + 1) * 2 * share]

    cand_cos = jnp.concatenate([cos_ref[prefix_len:, :]] * (rows // cand_len), axis=0)
    cand_sin = jnp.concatenate([sin_ref[prefix_len:, :]] * (rows // cand_len), axis=0)
    copies[3].wait()
    weights_of = [
        [w_query[rows_of(part * size, size), :] for part in parts]
    ] + [[v[pl.ds(0, size), :] for v in p] for p in pieces]

    def project(ks, first, count):
        made = None
        for i, part in enumerate(parts):
            weights = [weights_of[k][i] for k in ks]
            weights = weights[0] if len(ks) == 1 else jnp.concatenate(weights, axis=1)
            term = jnp.dot(
                normed[part, pl.ds(first, count), :], weights, preferred_element_type=jnp.float32
            )
            made = term if made is None else made + term
        return made

    def store(k, made, first, count):
        lower, upper = rotated(
            made[:, :half],
            made[:, half:],
            cand_cos[first : first + count],
            cand_sin[first : first + count],
        )
        q_ref[k, pl.ds(first, count), :half] = (lower * head ** (-0.5)).astype(jnp.bfloat16)
        q_ref[k, pl.ds(first, count), half:] = (upper * head ** (-0.5)).astype(jnp.bfloat16)

    for k in range(0, n - 1, 2):
        if k + 1 < n - 1:
            made = project((k, k + 1), 0, rows)
            store(k, made[:, :head], 0, rows)
            store(k + 1, made[:, head:], 0, rows)
        else:
            parts_made = [project((k,), at, rows // 2) for at in (0, rows // 2)]
            for at, made in zip((0, rows // 2), parts_made):
                store(k, made, at, rows // 2)


def last_kernel(dims, rounds, plan, *refs):
    n, rows, cand_len, _, prefix_len, _, head, _ = dims
    n_pieces = len(plan)
    normed, q_in, kv_in, cos_ref, sin_ref, len_ref, own_out = refs[:7]
    n_in = 7 + (n - 1) * n_pieces
    piece_refs = refs[7:n_in]
    o_ref = refs[n_in]
    w_out, kv_scr, heads, sem = refs[n_in + 1 :]
    me = lax.axis_index("tensor")
    parity = lax.rem(lax.axis_index("cand"), 2)
    half = head // 2
    share = kv_in.shape[2] // 2
    size = normed.shape[2]
    c = pltpu.make_async_copy(own_out, w_out, sem)
    c.start()
    sources, parts = places(rounds, plan, lax.axis_index("query"), me, parity)
    pieces = [piece_refs[r * n_pieces : (r + 1) * n_pieces] for r in range(n - 1)]
    cos, sin = cos_ref[...], sin_ref[...]
    cand_cos = jnp.concatenate([cos[prefix_len:]] * (rows // cand_len), axis=0)
    cand_sin = jnp.concatenate([sin[prefix_len:]] * (rows // cand_len), axis=0)
    all_cos = jnp.concatenate([cand_cos, cos[:prefix_len]], axis=0)
    all_sin = jnp.concatenate([cand_sin, sin[:prefix_len]], axis=0)

    last = pieces[-1]
    made = add_up(
        [
            lax.dot_general(
                normed[part],
                last[i][pl.ds(size + head, 2 * share), :],
                TRANS,
                preferred_element_type=jnp.float32,
            )
            for i, part in enumerate(parts)
        ]
    )
    for k, source in enumerate([me] + sources):
        kv_scr[source] = kv_in[k] if k < n - 1 else made.astype(jnp.bfloat16)
    made = add_up(
        [
            jnp.dot(
                normed[part, pl.ds(0, rows), :],
                last[i][pl.ds(0, size), :],
                preferred_element_type=jnp.float32,
            )
            for i, part in enumerate(parts)
        ]
    )
    lower, upper = rotated(made[:, :half], made[:, half:], cand_cos, cand_sin)
    last_q = jnp.concatenate([lower, upper], axis=1) * head ** (-0.5)
    last_q = last_q.astype(jnp.bfloat16)

    shares = [kv_scr[s] for s in range(n)]
    low = jnp.concatenate([p[:, :share] for p in shares[: n // 2]], axis=1).astype(jnp.float32)
    up = jnp.concatenate([p[:, :share] for p in shares[n // 2 :]], axis=1).astype(jnp.float32)
    keys = jnp.concatenate(rotated(low, up, all_cos, all_sin), axis=1).astype(jnp.bfloat16)
    values = jnp.concatenate([p[:, share:] for p in shares], axis=1)

    tall = (n, cand_len, cand_len + prefix_len)
    slot = lax.broadcasted_iota(jnp.int32, tall, 1).reshape(n * cand_len, tall[2])
    other = lax.broadcasted_iota(jnp.int32, tall, 2).reshape(n * cand_len, tall[2])
    seen = (slot >= other) | (other >= cand_len)
    for j in range(rows // cand_len):
        own = slice(j * cand_len, (j + 1) * cand_len)
        live = slot[:, :1] < len_ref[me * (rows // cand_len) + j]
        keys_j = jnp.concatenate([keys[own], keys[rows:]], axis=0)
        values_j = jnp.concatenate([values[own], values[rows:]], axis=0)
        queries = jnp.concatenate([q_in[k, own, :] for k in range(n - 1)] + [last_q[own]], axis=0)
        scores = lax.dot_general(queries, keys_j, TRANS, preferred_element_type=jnp.float32)
        scores = jnp.where(seen, scores, -jnp.inf)
        weights = jnp.exp(scores - scores.max(-1, keepdims=True))
        divisor = weights.sum(-1, keepdims=True)
        mix = jnp.dot(weights.astype(jnp.bfloat16), values_j, preferred_element_type=jnp.float32)
        mix = (mix * jnp.where(live, 1.0 / divisor, 0.0)).astype(jnp.bfloat16)
        for k in range(n):
            heads[k, own, :] = mix[k * cand_len : (k + 1) * cand_len]

    c.wait()
    for i in range(0, n_pieces, 2):
        spots = [rows_of(part * size, size) for part in parts[i : i + 2]]
        total = None
        for k in range(n):
            if k == 0:
                weights = [w_out[:, spot] for spot in spots]
            else:
                weights = [p[pl.ds(size, head), :] for p in pieces[k - 1][i : i + 2]]
            term = jnp.dot(
                heads[k], jnp.concatenate(weights, axis=1), preferred_element_type=jnp.float32
            )
            total = term if total is None else total + term
        for at, spot in enumerate(spots):
            o_ref[:, spot] = total[:, at * size : (at + 1) * size].astype(jnp.bfloat16)


def body(cand_states, prefix_states, norm_gain, w_query, w_key, w_value, w_out, cand_lengths):
    n = lax.axis_size("tensor")
    nq, nc = lax.axis_size("query"), lax.axis_size("cand")
    me = lax.axis_index("tensor")
    depth, head = w_query.shape
    share = w_key.shape[1]
    out_cols = w_out.shape[1]
    size = depth // (2 * nq)
    cand_len = cand_states.shape[0] // cand_lengths.shape[0]
    rows = cand_states.shape[0] // n
    prefix_len = prefix_states.shape[0] * nc
    half = head // 2
    any_spec = pl.BlockSpec(memory_space=pl.ANY)
    hbm = pl.BlockSpec(memory_space=pltpu.HBM)
    vmem = pl.BlockSpec(memory_space=pltpu.VMEM)
    smem = pl.BlockSpec(memory_space=pltpu.SMEM)

    key_t, value_t = w_key.T, w_value.T
    prefix_rows = prefix_states.shape[0]
    near = prefix_states
    if 2 * prefix_rows != prefix_len:
        near = lax.all_gather(prefix_states, "cand", axis=0, tiled=True)
    height = size + head + 2 * share
    tail = prefix_rows * (cand_states.shape[1] // size) if near is prefix_states else prefix_len
    piece = pl.pallas_call(
        functools.partial(cut_kernel, (prefix_rows, prefix_len, cand_states.shape[1])),
        name="cut",
        out_shape=jax.ShapeDtypeStruct((height + tail, size), jnp.bfloat16),
        in_specs=[any_spec] * 5,
        out_specs=vmem,
        scratch_shapes=[pltpu.SemaphoreType.DMA((8,))],
        compiler_params=pltpu.CompilerParams(vmem_limit_bytes=60 * 2**20),
    )(w_query, w_out, key_t, value_t, near)
    moved = along_line(piece, height)
    xs = [
        shift(k)(lax.dynamic_slice_in_dim(cand_states, (me + k) % n * rows, rows, 0))
        for k in range(1, n)
    ]
    across = other_core(piece)
    spreads = [spread(whole, v) for whole, v in moved]
    plan = tuple((masks, crossed) for _, masks, crossed in spreads[0])
    pieces = [v for s in spreads for v, _, _ in s]
    cos, sin = rotary_tables(prefix_len + cand_len, half, head)

    dims = (n, rows, cand_len, prefix_rows, prefix_len, depth, head, out_cols)
    count = len(spreads[0])
    every = rows + prefix_len
    early = pieces[: (n - 2) * count]
    last = pieces[(n - 2) * count :]
    normed, queries, pairs = pl.pallas_call(
        functools.partial(first_kernel, dims, nearest(n), plan),
        name="first",
        out_shape=[
            jax.ShapeDtypeStruct((depth // size, every, size), jnp.bfloat16),
            jax.ShapeDtypeStruct((n - 1, rows, head), jnp.bfloat16),
            jax.ShapeDtypeStruct((n - 1, every, 2 * share), jnp.bfloat16),
        ],
        in_specs=[hbm, vmem, vmem, vmem]
        + [vmem] * 4
        + [hbm] * 3
        + [vmem] * (len(xs) + len(early)),
        out_specs=[vmem] * 3,
        scratch_shapes=[
            pltpu.VMEM((rows, depth // n), jnp.bfloat16),
            pltpu.VMEM((depth, head), jnp.bfloat16),
            pltpu.VMEM((2 * share, depth), jnp.bfloat16),
            pltpu.VMEM((depth // size, prefix_len, size), jnp.bfloat16),
            pltpu.SemaphoreType.DMA((4,)),
        ],
        compiler_params=pltpu.CompilerParams(vmem_limit_bytes=24 * 2**20),
    )(
        cand_states, norm_gain.reshape(depth // size, 1, size), cos, sin,
        piece, across, last[0], last[count // 2],
        w_query, key_t, value_t, *xs, *early,
    )
    return pl.pallas_call(
        functools.partial(last_kernel, dims, nearest(n), plan),
        name="main",
        out_shape=jax.ShapeDtypeStruct((rows, out_cols), jnp.bfloat16),
        in_specs=[vmem] * 5 + [smem, hbm] + [vmem] * len(pieces),
        out_specs=vmem,
        scratch_shapes=[
            pltpu.VMEM((head, out_cols), jnp.bfloat16),
            pltpu.VMEM((n, every, 2 * share), jnp.bfloat16),
            pltpu.VMEM((n, rows, head), jnp.bfloat16),
            pltpu.SemaphoreType.DMA,
        ],
        compiler_params=pltpu.CompilerParams(vmem_limit_bytes=24 * 2**20),
    )(normed, queries, pairs, cos, sin, cand_lengths, w_out, *pieces)


def solution(mesh):
    in_specs = (
        P(("query", "cand"), "tensor"),
        P(("query", "cand"), "tensor"),
        P(),
        P(None, "tensor"),
        P(None, "tensor"),
        P(None, "tensor"),
        P("tensor", None),
        P(("query", "cand")),
    )
    out_specs = P(("query", "cand", "tensor"), None)

    return jax.shard_map(body, mesh=mesh, in_specs=in_specs, out_specs=out_specs, check_vma=False)
```

```python
import functools

import jax
import jax.numpy as jnp
from jax import lax
from jax.experimental import pallas as pl
from jax.experimental.pallas import tpu as pltpu
from jax.sharding import PartitionSpec as P


epsilon = 1e-06
theta_base = 10000.0
PLANE = ("query", "cand")
UNROLL = 4


def shift(k):
    n = lax.axis_size("tensor")
    return lambda v: lax.ppermute(v, "tensor", [(i, (i + k) % n) for i in range(n)])


def other_core(v):
    n = lax.axis_size("cand")
    return lax.ppermute(v, "cand", [(i, i ^ 1) for i in range(n)])


def plane_xor(masks):
    nq, nc = lax.axis_size("query"), lax.axis_size("cand")
    pairs = [(q * nc + c, (q ^ masks[c % 2]) * nc + c) for q in range(nq) for c in range(nc)]
    return lambda v: lax.ppermute(v, PLANE, pairs)


def spread(whole, piece):
    bits = lax.axis_size("query").bit_length() - 1
    held = [(piece, (0, 0))]
    for step in range(bits):
        flip = (1 << step, 1 << ((step + 1) % bits))
        held = held + [
            (
                plane_xor(flip)(v),
                (masks[0] ^ flip[0], masks[1] ^ flip[1]),
            )
            for v, masks in held
        ]
    held[0] = (whole, held[0][1])
    crossed = [(other_core(v), (masks[1], masks[0]), 1) for v, masks in held]
    return [(v, masks, 0) for v, masks in held] + crossed


def nearest(n):
    hops = [1] + [n - 1] * (n > 2) + list(range(2, n - 1))
    return [tuple((t - k) % n for t in range(n)) for k in hops]


def pick_kernel(choice, count, *refs):
    in_refs, o_refs = refs[:count], refs[count:]
    me = lax.axis_index("tensor")
    for i, ref in enumerate(in_refs):
        wanted = functools.reduce(
            jnp.logical_or, [me == t for t, which in enumerate(choice) if which == i]
        )

        @pl.when(wanted)
        def _(ref=ref):
            for o in o_refs:
                o[...] = ref[: o.shape[0], :]


def pick(by_place, heights, whole=None):
    distinct = []
    for v in by_place:
        if not any(v is d for d in distinct):
            distinct.append(v)
    choice = [next(i for i, d in enumerate(distinct) if d is v) for v in by_place]
    width = distinct[0].shape[1]
    made = pl.pallas_call(
        functools.partial(pick_kernel, choice, len(distinct)),
        out_shape=[jax.ShapeDtypeStruct((h, width), distinct[0].dtype) for h in heights],
        in_specs=[pl.BlockSpec(memory_space=pltpu.VMEM)] * len(distinct),
        out_specs=[pl.BlockSpec(memory_space=pltpu.VMEM)] * len(heights),
        compiler_params=pltpu.CompilerParams(vmem_limit_bytes=4 * 2**20),
    )(*distinct)
    return made if whole is None else [whole] + list(made)


def along_line(piece, height):
    n = lax.axis_size("tensor")
    came = {1: shift(1)(piece)}
    if n > 2:
        came[n - 1] = shift(n - 1)(piece)
    for k in range(2, n - 1):
        came[k] = shift(1)(came[k - 1])
    hops = [1] + [n - 1] * (n > 2) + list(range(2, n - 1))
    return [pick([came[k]] * n, (height,), came[k]) for k in hops]


def prefix_blocks(row, parity, prefix_rows, prefix_len, width, size):
    if 2 * prefix_rows == prefix_len:
        return [
            (row + i * prefix_rows, prefix_rows, parity * prefix_rows, i * size)
            for i in range(width // size)
        ]
    return [(row, prefix_len, 0, parity * size)]


def cut_kernel(dims, q_ref, out_ref, k_ref, v_ref, p_ref, o_ref, held, sems, out_sems):
    prefix_rows, prefix_len, width = dims
    size, head = o_ref.shape[1], out_ref.shape[0]
    share = k_ref.shape[0]
    parity = lax.rem(lax.axis_index("cand"), 2)
    part = (lax.axis_index("query") * 2 + parity) * size
    at = pl.ds(pl.multiple_of(part, size), size)
    copies, outs = [], []

    def copy(src, row, count):
        i = len(copies)
        spot = pl.ds(row, count)
        copies.append(pltpu.make_async_copy(src, held.at[spot, :], sems.at[i]))
        outs.append(pltpu.make_async_copy(held.at[spot, :], o_ref.at[spot, :], out_sems.at[i]))

    half, half_head = size // 2, head // 2
    for i in range(2):
        copy(q_ref.at[pl.ds(pl.multiple_of(part + i * half, half), half), :], i * half, half)
        copy(out_ref.at[pl.ds(i * half_head, half_head), at], size + i * half_head, half_head)
    copy(k_ref.at[:, at], size + head, share)
    copy(v_ref.at[:, at], size + head + share, share)
    blocks = prefix_blocks(size + head + 2 * share, parity, prefix_rows, prefix_len, width, size)
    for row, count, start, lane in blocks:
        if 2 * prefix_rows == prefix_len:
            start = 0
        lanes = pl.ds(pl.multiple_of(lane, size), size)
        copy(p_ref.at[pl.ds(start, count), lanes], row, count)
    for c in copies:
        c.start()
    for c, out in zip(copies, outs):
        c.wait()
        out.start()
    for out in outs:
        out.wait()


def rotary_tables(count, half, head_size):
    frequency = theta_base ** (-jnp.arange(half, dtype=jnp.float32) * 2.0 / head_size)
    angles = jnp.arange(count, dtype=jnp.float32)[:, None] * frequency[None, :]
    return jnp.cos(angles), jnp.sin(angles)


def rows_of(start, size):
    return pl.ds(pl.multiple_of(start, size), size)


def places(rounds, plan, q_at, me, parity):
    sources = []
    for by_place in rounds:
        value = by_place[0]
        for t in range(1, len(by_place)):
            value = jnp.where(me == t, by_place[t], value)
        sources.append(value)
    parts = []
    for masks, crossed in plan:
        mask = jnp.where(parity == 0, masks[0], masks[1])
        parts.append(lax.bitwise_xor(q_at, mask) * 2 + (parity if not crossed else 1 - parity))
    return sources, parts


def add_up(terms):
    chains = [functools.reduce(jnp.add, terms[i::2]) for i in range(2)]
    return chains[0] + chains[1]


def rotated(lower, upper, cos, sin):
    return lower * cos - upper * sin, upper * cos + lower * sin


TRANS = (((1,), (1,)), ((), ()))


def first_kernel(dims, rounds, plan, *refs):
    n, rows, cand_len, prefix_rows, prefix_len, depth, head, _ = dims
    n_pieces = len(plan)
    count = n - 2
    cand_ref, gain_ref, cos_ref, sin_ref = refs[:4]
    prefix_refs = refs[4:8]
    own_q, own_k, own_v = refs[8:11]
    x_refs = refs[11 : 11 + n - 1]
    n_in = 11 + n - 1 + count * n_pieces
    piece_refs = refs[11 + n - 1 : n_in]
    normed, q_ref, kv_ref = refs[n_in : n_in + 3]
    x_own, w_query, w_kv, p_raw, sems = refs[n_in + 3 :]
    me = lax.axis_index("tensor")
    parity = lax.rem(lax.axis_index("cand"), 2)
    width = depth // n
    half = head // 2
    share = own_k.shape[0]
    size = w_query.shape[1]
    chunks = width // size

    moves = [
        (cand_ref.at[rows_of(me * rows, rows), :], x_own),
        (own_k, w_kv.at[pl.ds(0, share), :]),
        (own_v, w_kv.at[pl.ds(share, share), :]),
        (own_q, w_query),
    ]
    copies = [pltpu.make_async_copy(src, dst, sems.at[i]) for i, (src, dst) in enumerate(moves)]
    for c in copies:
        c.start()
    sources, parts = places(rounds, plan, lax.axis_index("query"), me, parity)
    sources = [me] + sources
    pieces = [piece_refs[r * n_pieces : (r + 1) * n_pieces] for r in range(count)]

    fixed = size + head + 2 * share
    prefix_in = [prefix_refs[:2]] + [(p[0], p[n_pieces // 2]) for p in pieces] + [prefix_refs[2:]]
    for source, both in zip(sources, prefix_in):
        for ref, side in zip(both, (parity, 1 - parity)):
            for at, height, start, lane in prefix_blocks(
                fixed, side, prefix_rows, prefix_len, width, size
            ):
                whole = 2 * prefix_rows != prefix_len
                to = pl.ds(start, height) if whole else rows_of(start, height)
                p_raw[source * chunks + lane // size, to, :] = ref[pl.ds(at, height), :]

    block = 32

    def normalise(parts_in, to_rows):
        values = [ref[at].astype(jnp.float32) for _, ref, at in parts_in]
        square = sum(v * v for v in values)
        square = jnp.sum(square, axis=-1, keepdims=True) / depth
        scale = lax.rsqrt(square + epsilon)
        for (chunk, ref, at), v in zip(parts_in, values):
            normed[chunk, to_rows, :] = (v * scale * gain_ref[chunk]).astype(jnp.bfloat16)

    def prefix_block(i, carry):
        at = rows_of(i * block, block)
        to = pl.ds(pl.multiple_of(rows + i * block, block), block)
        normalise([(c, p_raw, (c, at, slice(None))) for c in range(n * chunks)], to)
        return carry

    lax.fori_loop(0, prefix_len // block, prefix_block, 0, unroll=UNROLL)
    copies[0].wait()
    x_from = [me] + [lax.rem(me - k + n, n) for k in range(1, n)]

    def cand_block(i, carry):
        at = rows_of(i * block, block)
        normalise(
            [
                (source * chunks + h, ref, (at, pl.ds(h * size, size)))
                for source, ref in zip(x_from, [x_own] + list(x_refs))
                for h in range(chunks)
            ],
            at,
        )
        return carry

    lax.fori_loop(0, rows // block, cand_block, 0, unroll=UNROLL)

    for c in copies[1:3]:
        c.wait()
    made = []
    for i, part in enumerate(parts):
        weights = jnp.concatenate(
            [w_kv[:, rows_of(part * size, size)]]
            + [p[i][pl.ds(size + head, 2 * share), :] for p in pieces],
            axis=0,
        )
        made.append(
            lax.dot_general(normed[part], weights, TRANS, preferred_element_type=jnp.float32)
        )
    made = functools.reduce(jnp.add, made).astype(jnp.bfloat16)
    for k in range(n - 1):
        kv_ref[k] = made[:, k * 2 * share : (k + 1) * 2 * share]

    cand_cos = jnp.concatenate([cos_ref[prefix_len:, :]] * (rows // cand_len), axis=0)
    cand_sin = jnp.concatenate([sin_ref[prefix_len:, :]] * (rows // cand_len), axis=0)
    copies[3].wait()
    weights_of = [
        [w_query[rows_of(part * size, size), :] for part in parts]
    ] + [[v[pl.ds(0, size), :] for v in p] for p in pieces]

    def project(ks, first, count):
        made = None
        for i, part in enumerate(parts):
            weights = [weights_of[k][i] for k in ks]
            weights = weights[0] if len(ks) == 1 else jnp.concatenate(weights, axis=1)
            term = jnp.dot(
                normed[part, pl.ds(first, count), :], weights, preferred_element_type=jnp.float32
            )
            made = term if made is None else made + term
        return made

    def store(k, made, first, count):
        lower, upper = rotated(
            made[:, :half],
            made[:, half:],
            cand_cos[first : first + count],
            cand_sin[first : first + count],
        )
        q_ref[k, pl.ds(first, count), :half] = (lower * head ** (-0.5)).astype(jnp.bfloat16)
        q_ref[k, pl.ds(first, count), half:] = (upper * head ** (-0.5)).astype(jnp.bfloat16)

    for k in range(0, n - 1, 2):
        if k + 1 < n - 1:
            made = project((k, k + 1), 0, rows)
            store(k, made[:, :head], 0, rows)
            store(k + 1, made[:, head:], 0, rows)
        else:
            parts_made = [project((k,), at, rows // 2) for at in (0, rows // 2)]
            for at, made in zip((0, rows // 2), parts_made):
                store(k, made, at, rows // 2)


def late(count):
    return (count // 2 - 1, count - 1)


def second_kernel(dims, rounds, plan, *refs):
    n, rows, _, _, _, _, head, _ = dims
    share2 = 2 * (head // n)
    normed, piece_refs, q_ref, kv_ref = refs[0], refs[1:-2], refs[-2], refs[-1]
    me = lax.axis_index("tensor")
    parity = lax.rem(lax.axis_index("cand"), 2)
    size = normed.shape[2]
    _, parts = places(rounds, plan, lax.axis_index("query"), me, parity)
    parts = [part for i, part in enumerate(parts) if i not in late(len(plan))]
    kv_ref[...] = add_up(
        [
            lax.dot_general(
                normed[part],
                ref[pl.ds(size + head, share2), :],
                TRANS,
                preferred_element_type=jnp.float32,
            )
            for part, ref in zip(parts, piece_refs)
        ]
    )
    q_ref[...] = add_up(
        [
            jnp.dot(
                normed[part, pl.ds(0, rows), :],
                ref[pl.ds(0, size), :],
                preferred_element_type=jnp.float32,
            )
            for part, ref in zip(parts, piece_refs)
        ]
    )


def last_kernel(dims, rounds, plan, *refs):
    n, rows, cand_len, _, prefix_len, _, head, _ = dims
    n_pieces = len(plan)
    normed, q_in, kv_in, cos_ref, sin_ref, len_ref, own_out, q_part, kv_part = refs[:9]
    n_in = 9 + (n - 1) * n_pieces
    piece_refs = refs[9:n_in]
    o_ref = refs[n_in]
    w_out, kv_scr, heads, sem = refs[n_in + 1 :]
    me = lax.axis_index("tensor")
    parity = lax.rem(lax.axis_index("cand"), 2)
    half = head // 2
    share = kv_in.shape[2] // 2
    size = normed.shape[2]
    c = pltpu.make_async_copy(own_out, w_out, sem)
    c.start()
    sources, parts = places(rounds, plan, lax.axis_index("query"), me, parity)
    pieces = [piece_refs[r * n_pieces : (r + 1) * n_pieces] for r in range(n - 1)]
    cos, sin = cos_ref[...], sin_ref[...]
    cand_cos = jnp.concatenate([cos[prefix_len:]] * (rows // cand_len), axis=0)
    cand_sin = jnp.concatenate([sin[prefix_len:]] * (rows // cand_len), axis=0)
    all_cos = jnp.concatenate([cand_cos, cos[:prefix_len]], axis=0)
    all_sin = jnp.concatenate([cand_sin, sin[:prefix_len]], axis=0)

    last = [(parts[i], pieces[-1][i]) for i in late(n_pieces)]
    made = kv_part[...] + add_up(
        [
            lax.dot_general(
                normed[part],
                ref[pl.ds(size + head, 2 * share), :],
                TRANS,
                preferred_element_type=jnp.float32,
            )
            for part, ref in last
        ]
    )
    for k, source in enumerate([me] + sources):
        kv_scr[source] = kv_in[k] if k < n - 1 else made.astype(jnp.bfloat16)
    made = q_part[...] + add_up(
        [
            jnp.dot(
                normed[part, pl.ds(0, rows), :],
                ref[pl.ds(0, size), :],
                preferred_element_type=jnp.float32,
            )
            for part, ref in last
        ]
    )
    lower, upper = rotated(made[:, :half], made[:, half:], cand_cos, cand_sin)
    last_q = jnp.concatenate([lower, upper], axis=1) * head ** (-0.5)
    last_q = last_q.astype(jnp.bfloat16)

    shares = [kv_scr[s] for s in range(n)]
    low = jnp.concatenate([p[:, :share] for p in shares[: n // 2]], axis=1).astype(jnp.float32)
    up = jnp.concatenate([p[:, :share] for p in shares[n // 2 :]], axis=1).astype(jnp.float32)
    keys = jnp.concatenate(rotated(low, up, all_cos, all_sin), axis=1).astype(jnp.bfloat16)
    values = jnp.concatenate([p[:, share:] for p in shares], axis=1)

    group = min(2, n)
    tall = (group, cand_len, cand_len + prefix_len)
    slot = lax.broadcasted_iota(jnp.int32, tall, 1).reshape(group * cand_len, tall[2])
    other = lax.broadcasted_iota(jnp.int32, tall, 2).reshape(group * cand_len, tall[2])
    seen = (slot >= other) | (other >= cand_len)
    for j in range(rows // cand_len):
        own = slice(j * cand_len, (j + 1) * cand_len)
        live = slot[:, :1] < len_ref[me * (rows // cand_len) + j]
        keys_j = jnp.concatenate([keys[own], keys[rows:]], axis=0)
        values_j = jnp.concatenate([values[own], values[rows:]], axis=0)
        for g in range(0, n, group):
            heads_g = range(g, g + group)
            queries = [q_in[k, own, :] if k < n - 1 else last_q[own] for k in heads_g]
            queries = jnp.concatenate(queries, axis=0) if group > 1 else queries[0]
            scores = lax.dot_general(queries, keys_j, TRANS, preferred_element_type=jnp.float32)
            scores = jnp.where(seen, scores, -jnp.inf)
            weights = jnp.exp(scores - scores.max(-1, keepdims=True))
            divisor = weights.sum(-1, keepdims=True)
            mix = jnp.dot(
                weights.astype(jnp.bfloat16), values_j, preferred_element_type=jnp.float32
            )
            mix = (mix * jnp.where(live, 1.0 / divisor, 0.0)).astype(jnp.bfloat16)
            for at, k in enumerate(heads_g):
                heads[k, own, :] = mix[at * cand_len : (at + 1) * cand_len]

    c.wait()
    for i in range(0, n_pieces, 2):
        spots = [rows_of(part * size, size) for part in parts[i : i + 2]]
        total = None
        for k in range(n):
            if k == 0:
                weights = [w_out[:, spot] for spot in spots]
            else:
                weights = [p[pl.ds(size, head), :] for p in pieces[k - 1][i : i + 2]]
            term = jnp.dot(
                heads[k], jnp.concatenate(weights, axis=1), preferred_element_type=jnp.float32
            )
            total = term if total is None else total + term
        for at, spot in enumerate(spots):
            o_ref[:, spot] = total[:, at * size : (at + 1) * size].astype(jnp.bfloat16)


def body(cand_states, prefix_states, norm_gain, w_query, w_key, w_value, w_out, cand_lengths):
    n = lax.axis_size("tensor")
    nq, nc = lax.axis_size("query"), lax.axis_size("cand")
    me = lax.axis_index("tensor")
    depth, head = w_query.shape
    share = w_key.shape[1]
    out_cols = w_out.shape[1]
    size = depth // (2 * nq)
    cand_len = cand_states.shape[0] // cand_lengths.shape[0]
    rows = cand_states.shape[0] // n
    prefix_len = prefix_states.shape[0] * nc
    half = head // 2
    any_spec = pl.BlockSpec(memory_space=pl.ANY)
    hbm = pl.BlockSpec(memory_space=pltpu.HBM)
    vmem = pl.BlockSpec(memory_space=pltpu.VMEM)
    smem = pl.BlockSpec(memory_space=pltpu.SMEM)

    key_t, value_t = w_key.T, w_value.T
    prefix_rows = prefix_states.shape[0]
    near = prefix_states
    if 2 * prefix_rows != prefix_len:
        near = lax.all_gather(prefix_states, "cand", axis=0, tiled=True)
    height = size + head + 2 * share
    tail = prefix_rows * (cand_states.shape[1] // size) if near is prefix_states else prefix_len
    piece = pl.pallas_call(
        functools.partial(cut_kernel, (prefix_rows, prefix_len, cand_states.shape[1])),
        name="cut",
        out_shape=jax.ShapeDtypeStruct((height + tail, size), jnp.bfloat16),
        in_specs=[any_spec] * 5,
        out_specs=any_spec,
        scratch_shapes=[
            pltpu.VMEM((height + tail, size), jnp.bfloat16),
            pltpu.SemaphoreType.DMA((8,)),
            pltpu.SemaphoreType.DMA((8,)),
        ],
        compiler_params=pltpu.CompilerParams(vmem_limit_bytes=60 * 2**20),
    )(w_query, w_out, key_t, value_t, near)
    moved = along_line(piece, height)
    xs = [
        shift(k)(lax.dynamic_slice_in_dim(cand_states, (me + k) % n * rows, rows, 0))
        for k in range(1, n)
    ]
    across = other_core(piece)
    spreads = [spread(whole, v) for whole, v in moved]
    plan = tuple((masks, crossed) for _, masks, crossed in spreads[0])
    pieces = [v for s in spreads for v, _, _ in s]
    cos, sin = rotary_tables(prefix_len + cand_len, half, head)

    dims = (n, rows, cand_len, prefix_rows, prefix_len, depth, head, out_cols)
    count = len(spreads[0])
    every = rows + prefix_len
    early = pieces[: (n - 2) * count]
    last = pieces[(n - 2) * count :]
    normed, queries, pairs = pl.pallas_call(
        functools.partial(first_kernel, dims, nearest(n), plan),
        name="first",
        out_shape=[
            jax.ShapeDtypeStruct((depth // size, every, size), jnp.bfloat16),
            jax.ShapeDtypeStruct((n - 1, rows, head), jnp.bfloat16),
            jax.ShapeDtypeStruct((n - 1, every, 2 * share), jnp.bfloat16),
        ],
        in_specs=[hbm, vmem, vmem, vmem]
        + [vmem] * 4
        + [hbm] * 3
        + [vmem] * (len(xs) + len(early)),
        out_specs=[vmem] * 3,
        scratch_shapes=[
            pltpu.VMEM((rows, depth // n), jnp.bfloat16),
            pltpu.VMEM((depth, head), jnp.bfloat16),
            pltpu.VMEM((2 * share, depth), jnp.bfloat16),
            pltpu.VMEM((depth // size, prefix_len, size), jnp.bfloat16),
            pltpu.SemaphoreType.DMA((4,)),
        ],
        compiler_params=pltpu.CompilerParams(vmem_limit_bytes=24 * 2**20),
    )(
        cand_states, norm_gain.reshape(depth // size, 1, size), cos, sin,
        piece, across, last[0], last[count // 2],
        w_query, key_t, value_t, *xs, *early,
    )
    q_part, kv_part = pl.pallas_call(
        functools.partial(second_kernel, dims, nearest(n), plan),
        name="second",
        out_shape=[
            jax.ShapeDtypeStruct((rows, head), jnp.float32),
            jax.ShapeDtypeStruct((every, 2 * share), jnp.float32),
        ],
        in_specs=[vmem] * (1 + count - 2),
        out_specs=[vmem] * 2,
        compiler_params=pltpu.CompilerParams(vmem_limit_bytes=16 * 2**20),
    )(normed, *[v for i, v in enumerate(last) if i not in late(count)])
    return pl.pallas_call(
        functools.partial(last_kernel, dims, nearest(n), plan),
        name="main",
        out_shape=jax.ShapeDtypeStruct((rows, out_cols), jnp.bfloat16),
        in_specs=[vmem] * 5 + [smem, hbm] + [vmem] * (2 + len(pieces)),
        out_specs=vmem,
        scratch_shapes=[
            pltpu.VMEM((head, out_cols), jnp.bfloat16),
            pltpu.VMEM((n, every, 2 * share), jnp.bfloat16),
            pltpu.VMEM((n, rows, head), jnp.bfloat16),
            pltpu.SemaphoreType.DMA,
        ],
        compiler_params=pltpu.CompilerParams(vmem_limit_bytes=24 * 2**20),
    )(normed, queries, pairs, cos, sin, cand_lengths, w_out, q_part, kv_part, *pieces)


def solution(mesh):
    in_specs = (
        P(("query", "cand"), "tensor"),
        P(("query", "cand"), "tensor"),
        P(),
        P(None, "tensor"),
        P(None, "tensor"),
        P(None, "tensor"),
        P("tensor", None),
        P(("query", "cand")),
    )
    out_specs = P(("query", "cand", "tensor"), None)

    return jax.shard_map(body, mesh=mesh, in_specs=in_specs, out_specs=out_specs, check_vma=False)
```

```python
import functools

import jax
import jax.numpy as jnp
from jax import lax
from jax.experimental import pallas as pl
from jax.experimental.pallas import tpu as pltpu
from jax.sharding import PartitionSpec as P


epsilon = 1e-06
theta_base = 10000.0
PLANE = ("query", "cand")
UNROLL = 8


def shift(k):
    n = lax.axis_size("tensor")
    return lambda v: lax.ppermute(v, "tensor", [(i, (i + k) % n) for i in range(n)])


def other_core(v):
    n = lax.axis_size("cand")
    return lax.ppermute(v, "cand", [(i, i ^ 1) for i in range(n)])


def plane_xor(masks):
    nq, nc = lax.axis_size("query"), lax.axis_size("cand")
    pairs = [(q * nc + c, (q ^ masks[c % 2]) * nc + c) for q in range(nq) for c in range(nc)]
    return lambda v: lax.ppermute(v, PLANE, pairs)


def spread(whole, piece):
    bits = lax.axis_size("query").bit_length() - 1
    held = [(piece, (0, 0))]
    for step in range(bits):
        flip = (1 << step, 1 << ((step + 1) % bits))
        held = held + [
            (
                plane_xor(flip)(v),
                (masks[0] ^ flip[0], masks[1] ^ flip[1]),
            )
            for v, masks in held
        ]
    held[0] = (whole, held[0][1])
    crossed = [(other_core(v), (masks[1], masks[0]), 1) for v, masks in held]
    return [(v, masks, 0) for v, masks in held] + crossed


def nearest(n):
    hops = [1] + [n - 1] * (n > 2) + list(range(2, n - 1))
    return [tuple((t - k) % n for t in range(n)) for k in hops]


def pick_kernel(choice, count, *refs):
    in_refs, o_refs = refs[:count], refs[count:]
    me = lax.axis_index("tensor")
    for i, ref in enumerate(in_refs):
        wanted = functools.reduce(
            jnp.logical_or, [me == t for t, which in enumerate(choice) if which == i]
        )

        @pl.when(wanted)
        def _(ref=ref):
            for o in o_refs:
                o[...] = ref[: o.shape[0], :]


def pick(by_place, heights, whole=None):
    distinct = []
    for v in by_place:
        if not any(v is d for d in distinct):
            distinct.append(v)
    choice = [next(i for i, d in enumerate(distinct) if d is v) for v in by_place]
    width = distinct[0].shape[1]
    made = pl.pallas_call(
        functools.partial(pick_kernel, choice, len(distinct)),
        out_shape=[jax.ShapeDtypeStruct((h, width), distinct[0].dtype) for h in heights],
        in_specs=[pl.BlockSpec(memory_space=pltpu.VMEM)] * len(distinct),
        out_specs=[pl.BlockSpec(memory_space=pltpu.VMEM)] * len(heights),
        compiler_params=pltpu.CompilerParams(vmem_limit_bytes=4 * 2**20),
    )(*distinct)
    return made if whole is None else [whole] + list(made)


def along_line(piece, height):
    n = lax.axis_size("tensor")
    came = {1: shift(1)(piece)}
    if n > 2:
        came[n - 1] = shift(n - 1)(piece)
    for k in range(2, n - 1):
        came[k] = shift(1)(came[k - 1])
    hops = [1] + [n - 1] * (n > 2) + list(range(2, n - 1))
    return [pick([came[k]] * n, (height,), came[k]) for k in hops]


def prefix_blocks(row, parity, prefix_rows, prefix_len, width, size):
    if 2 * prefix_rows == prefix_len:
        return [
            (row + i * prefix_rows, prefix_rows, parity * prefix_rows, i * size)
            for i in range(width // size)
        ]
    return [(row, prefix_len, 0, parity * size)]


def cut_kernel(dims, q_ref, out_ref, k_ref, v_ref, p_ref, o_ref, held, sems, out_sems):
    prefix_rows, prefix_len, width = dims
    size, head = o_ref.shape[1], out_ref.shape[0]
    share = k_ref.shape[0]
    parity = lax.rem(lax.axis_index("cand"), 2)
    part = (lax.axis_index("query") * 2 + parity) * size
    at = pl.ds(pl.multiple_of(part, size), size)
    copies, outs = [], []

    def copy(src, row, count):
        i = len(copies)
        spot = pl.ds(row, count)
        copies.append(pltpu.make_async_copy(src, held.at[spot, :], sems.at[i]))
        outs.append(pltpu.make_async_copy(held.at[spot, :], o_ref.at[spot, :], out_sems.at[i]))

    half, half_head = size // 2, head // 2
    for i in range(2):
        copy(q_ref.at[pl.ds(pl.multiple_of(part + i * half, half), half), :], i * half, half)
        copy(out_ref.at[pl.ds(i * half_head, half_head), at], size + i * half_head, half_head)
    copy(k_ref.at[:, at], size + head, share)
    copy(v_ref.at[:, at], size + head + share, share)
    blocks = prefix_blocks(size + head + 2 * share, parity, prefix_rows, prefix_len, width, size)
    for row, count, start, lane in blocks:
        if 2 * prefix_rows == prefix_len:
            start = 0
        lanes = pl.ds(pl.multiple_of(lane, size), size)
        copy(p_ref.at[pl.ds(start, count), lanes], row, count)
    for c in copies:
        c.start()
    for c, out in zip(copies, outs):
        c.wait()
        out.start()
    for out in outs:
        out.wait()


def rotary_tables(count, half, head_size):
    frequency = theta_base ** (-jnp.arange(half, dtype=jnp.float32) * 2.0 / head_size)
    angles = jnp.arange(count, dtype=jnp.float32)[:, None] * frequency[None, :]
    return jnp.cos(angles), jnp.sin(angles)


def rows_of(start, size):
    return pl.ds(pl.multiple_of(start, size), size)


def places(rounds, plan, q_at, me, parity):
    sources = []
    for by_place in rounds:
        value = by_place[0]
        for t in range(1, len(by_place)):
            value = jnp.where(me == t, by_place[t], value)
        sources.append(value)
    parts = []
    for masks, crossed in plan:
        mask = jnp.where(parity == 0, masks[0], masks[1])
        parts.append(lax.bitwise_xor(q_at, mask) * 2 + (parity if not crossed else 1 - parity))
    return sources, parts


def add_up(terms):
    chains = [functools.reduce(jnp.add, terms[i::2]) for i in range(2)]
    return chains[0] + chains[1]


def rotated(lower, upper, cos, sin):
    return lower * cos - upper * sin, upper * cos + lower * sin


TRANS = (((1,), (1,)), ((), ()))


def first_kernel(dims, rounds, plan, *refs):
    n, rows, cand_len, prefix_rows, prefix_len, depth, head, _ = dims
    n_pieces = len(plan)
    count = n - 2
    cand_ref, gain_ref, cos_ref, sin_ref = refs[:4]
    prefix_refs = refs[4:8]
    own_q, own_k, own_v = refs[8:11]
    x_refs = refs[11 : 11 + n - 1]
    n_in = 11 + n - 1 + count * n_pieces
    piece_refs = refs[11 + n - 1 : n_in]
    normed, q_ref, kv_ref = refs[n_in : n_in + 3]
    x_own, w_query, w_kv, p_raw, sems = refs[n_in + 3 :]
    me = lax.axis_index("tensor")
    parity = lax.rem(lax.axis_index("cand"), 2)
    width = depth // n
    half = head // 2
    share = own_k.shape[0]
    size = w_query.shape[1]
    chunks = width // size

    moves = [
        (cand_ref.at[rows_of(me * rows, rows), :], x_own),
        (own_k, w_kv.at[pl.ds(0, share), :]),
        (own_v, w_kv.at[pl.ds(share, share), :]),
        (own_q, w_query),
    ]
    copies = [pltpu.make_async_copy(src, dst, sems.at[i]) for i, (src, dst) in enumerate(moves)]
    for c in copies:
        c.start()
    sources, parts = places(rounds, plan, lax.axis_index("query"), me, parity)
    sources = [me] + sources
    pieces = [piece_refs[r * n_pieces : (r + 1) * n_pieces] for r in range(count)]

    fixed = size + head + 2 * share
    prefix_in = [prefix_refs[:2]] + [(p[0], p[n_pieces // 2]) for p in pieces] + [prefix_refs[2:]]
    for source, both in zip(sources, prefix_in):
        for ref, side in zip(both, (parity, 1 - parity)):
            for at, height, start, lane in prefix_blocks(
                fixed, side, prefix_rows, prefix_len, width, size
            ):
                whole = 2 * prefix_rows != prefix_len
                to = pl.ds(start, height) if whole else rows_of(start, height)
                p_raw[source * chunks + lane // size, to, :] = ref[pl.ds(at, height), :]

    block = 32

    def normalise(parts_in, to_rows):
        values = [ref[at].astype(jnp.float32) for _, ref, at in parts_in]
        square = sum(v * v for v in values)
        square = jnp.sum(square, axis=-1, keepdims=True) / depth
        scale = lax.rsqrt(square + epsilon)
        for (chunk, ref, at), v in zip(parts_in, values):
            normed[chunk, to_rows, :] = (v * scale * gain_ref[chunk]).astype(jnp.bfloat16)

    def prefix_block(i, carry):
        at = rows_of(i * block, block)
        to = pl.ds(pl.multiple_of(rows + i * block, block), block)
        normalise([(c, p_raw, (c, at, slice(None))) for c in range(n * chunks)], to)
        return carry

    lax.fori_loop(0, prefix_len // block, prefix_block, 0, unroll=UNROLL)
    copies[0].wait()
    x_from = [me] + [lax.rem(me - k + n, n) for k in range(1, n)]

    def cand_block(i, carry):
        at = rows_of(i * block, block)
        normalise(
            [
                (source * chunks + h, ref, (at, pl.ds(h * size, size)))
                for source, ref in zip(x_from, [x_own] + list(x_refs))
                for h in range(chunks)
            ],
            at,
        )
        return carry

    lax.fori_loop(0, rows // block, cand_block, 0, unroll=UNROLL)

    for c in copies[1:3]:
        c.wait()
    made = []
    for i, part in enumerate(parts):
        weights = jnp.concatenate(
            [w_kv[:, rows_of(part * size, size)]]
            + [p[i][pl.ds(size + head, 2 * share), :] for p in pieces],
            axis=0,
        )
        made.append(
            lax.dot_general(normed[part], weights, TRANS, preferred_element_type=jnp.float32)
        )
    made = functools.reduce(jnp.add, made).astype(jnp.bfloat16)
    for k in range(n - 1):
        kv_ref[k] = made[:, k * 2 * share : (k + 1) * 2 * share]

    cand_cos = jnp.concatenate([cos_ref[prefix_len:, :]] * (rows // cand_len), axis=0)
    cand_sin = jnp.concatenate([sin_ref[prefix_len:, :]] * (rows // cand_len), axis=0)
    copies[3].wait()
    weights_of = [
        [w_query[rows_of(part * size, size), :] for part in parts]
    ] + [[v[pl.ds(0, size), :] for v in p] for p in pieces]

    def project(ks, first, count):
        made = None
        for i, part in enumerate(parts):
            weights = [weights_of[k][i] for k in ks]
            weights = weights[0] if len(ks) == 1 else jnp.concatenate(weights, axis=1)
            term = jnp.dot(
                normed[part, pl.ds(first, count), :], weights, preferred_element_type=jnp.float32
            )
            made = term if made is None else made + term
        return made

    def store(k, made, first, count):
        lower, upper = rotated(
            made[:, :half],
            made[:, half:],
            cand_cos[first : first + count],
            cand_sin[first : first + count],
        )
        q_ref[k, pl.ds(first, count), :half] = (lower * head ** (-0.5)).astype(jnp.bfloat16)
        q_ref[k, pl.ds(first, count), half:] = (upper * head ** (-0.5)).astype(jnp.bfloat16)

    for k in range(0, n - 1, 2):
        if k + 1 < n - 1:
            made = project((k, k + 1), 0, rows)
            store(k, made[:, :head], 0, rows)
            store(k + 1, made[:, head:], 0, rows)
        else:
            parts_made = [project((k,), at, rows // 2) for at in (0, rows // 2)]
            for at, made in zip((0, rows // 2), parts_made):
                store(k, made, at, rows // 2)


def late(count):
    return (count // 2 - 1, count - 1)


def second_kernel(dims, rounds, plan, *refs):
    n, rows, _, _, _, _, head, _ = dims
    share2 = 2 * (head // n)
    normed, piece_refs, q_ref, kv_ref = refs[0], refs[1:-2], refs[-2], refs[-1]
    me = lax.axis_index("tensor")
    parity = lax.rem(lax.axis_index("cand"), 2)
    size = normed.shape[2]
    _, parts = places(rounds, plan, lax.axis_index("query"), me, parity)
    parts = [part for i, part in enumerate(parts) if i not in late(len(plan))]
    kv_ref[...] = add_up(
        [
            lax.dot_general(
                normed[part],
                ref[pl.ds(size + head, share2), :],
                TRANS,
                preferred_element_type=jnp.float32,
            )
            for part, ref in zip(parts, piece_refs)
        ]
    )
    q_ref[...] = add_up(
        [
            jnp.dot(
                normed[part, pl.ds(0, rows), :],
                ref[pl.ds(0, size), :],
                preferred_element_type=jnp.float32,
            )
            for part, ref in zip(parts, piece_refs)
        ]
    )


def last_kernel(dims, rounds, plan, *refs):
    n, rows, cand_len, _, prefix_len, _, head, _ = dims
    n_pieces = len(plan)
    normed, q_in, kv_in, cos_ref, sin_ref, len_ref, own_out, q_part, kv_part = refs[:9]
    n_in = 9 + (n - 1) * n_pieces
    piece_refs = refs[9:n_in]
    o_ref = refs[n_in]
    w_out, kv_scr, heads, made_out, sem, out_sems = refs[n_in + 1 :]
    me = lax.axis_index("tensor")
    parity = lax.rem(lax.axis_index("cand"), 2)
    half = head // 2
    share = kv_in.shape[2] // 2
    size = normed.shape[2]
    c = pltpu.make_async_copy(own_out, w_out, sem)
    c.start()
    sources, parts = places(rounds, plan, lax.axis_index("query"), me, parity)
    pieces = [piece_refs[r * n_pieces : (r + 1) * n_pieces] for r in range(n - 1)]
    cos, sin = cos_ref[...], sin_ref[...]
    cand_cos = jnp.concatenate([cos[prefix_len:]] * (rows // cand_len), axis=0)
    cand_sin = jnp.concatenate([sin[prefix_len:]] * (rows // cand_len), axis=0)
    all_cos = jnp.concatenate([cand_cos, cos[:prefix_len]], axis=0)
    all_sin = jnp.concatenate([cand_sin, sin[:prefix_len]], axis=0)

    last = [(parts[i], pieces[-1][i]) for i in late(n_pieces)]
    made = kv_part[...] + add_up(
        [
            lax.dot_general(
                normed[part],
                ref[pl.ds(size + head, 2 * share), :],
                TRANS,
                preferred_element_type=jnp.float32,
            )
            for part, ref in last
        ]
    )
    for k, source in enumerate([me] + sources):
        kv_scr[source] = kv_in[k] if k < n - 1 else made.astype(jnp.bfloat16)
    made = q_part[...] + add_up(
        [
            jnp.dot(
                normed[part, pl.ds(0, rows), :],
                ref[pl.ds(0, size), :],
                preferred_element_type=jnp.float32,
            )
            for part, ref in last
        ]
    )
    lower, upper = rotated(made[:, :half], made[:, half:], cand_cos, cand_sin)
    last_q = jnp.concatenate([lower, upper], axis=1) * head ** (-0.5)
    last_q = last_q.astype(jnp.bfloat16)

    shares = [kv_scr[s] for s in range(n)]
    low = jnp.concatenate([p[:, :share] for p in shares[: n // 2]], axis=1).astype(jnp.float32)
    up = jnp.concatenate([p[:, :share] for p in shares[n // 2 :]], axis=1).astype(jnp.float32)
    keys = jnp.concatenate(rotated(low, up, all_cos, all_sin), axis=1).astype(jnp.bfloat16)
    values = jnp.concatenate([p[:, share:] for p in shares], axis=1)

    group = min(2, n)
    tall = (group, cand_len, cand_len + prefix_len)
    slot = lax.broadcasted_iota(jnp.int32, tall, 1).reshape(group * cand_len, tall[2])
    other = lax.broadcasted_iota(jnp.int32, tall, 2).reshape(group * cand_len, tall[2])
    seen = (slot >= other) | (other >= cand_len)
    for j in range(rows // cand_len):
        own = slice(j * cand_len, (j + 1) * cand_len)
        live = slot[:, :1] < len_ref[me * (rows // cand_len) + j]
        keys_j = jnp.concatenate([keys[own], keys[rows:]], axis=0)
        values_j = jnp.concatenate([values[own], values[rows:]], axis=0)
        for g in range(0, n, group):
            heads_g = range(g, g + group)
            queries = [q_in[k, own, :] if k < n - 1 else last_q[own] for k in heads_g]
            queries = jnp.concatenate(queries, axis=0) if group > 1 else queries[0]
            scores = lax.dot_general(queries, keys_j, TRANS, preferred_element_type=jnp.float32)
            scores = jnp.where(seen, scores, -jnp.inf)
            weights = jnp.exp(scores - scores.max(-1, keepdims=True))
            divisor = weights.sum(-1, keepdims=True)
            mix = jnp.dot(
                weights.astype(jnp.bfloat16), values_j, preferred_element_type=jnp.float32
            )
            mix = (mix * jnp.where(live, 1.0 / divisor, 0.0)).astype(jnp.bfloat16)
            for at, k in enumerate(heads_g):
                heads[k, own, :] = mix[at * cand_len : (at + 1) * cand_len]

    c.wait()
    outs = []
    for i in range(0, n_pieces, 2):
        spots = [rows_of(part * size, size) for part in parts[i : i + 2]]
        total = None
        for k in range(n):
            if k == 0:
                weights = [w_out[:, spot] for spot in spots]
            else:
                weights = [p[pl.ds(size, head), :] for p in pieces[k - 1][i : i + 2]]
            term = jnp.dot(
                heads[k], jnp.concatenate(weights, axis=1), preferred_element_type=jnp.float32
            )
            total = term if total is None else total + term
        for at, spot in enumerate(spots):
            made_out[i + at] = total[:, at * size : (at + 1) * size].astype(jnp.bfloat16)
            out = pltpu.make_async_copy(made_out.at[i + at], o_ref.at[:, spot], out_sems.at[i + at])
            out.start()
            outs.append(out)
    for out in outs:
        out.wait()


def body(cand_states, prefix_states, norm_gain, w_query, w_key, w_value, w_out, cand_lengths):
    n = lax.axis_size("tensor")
    nq, nc = lax.axis_size("query"), lax.axis_size("cand")
    me = lax.axis_index("tensor")
    depth, head = w_query.shape
    share = w_key.shape[1]
    out_cols = w_out.shape[1]
    size = depth // (2 * nq)
    cand_len = cand_states.shape[0] // cand_lengths.shape[0]
    rows = cand_states.shape[0] // n
    prefix_len = prefix_states.shape[0] * nc
    half = head // 2
    any_spec = pl.BlockSpec(memory_space=pl.ANY)
    hbm = pl.BlockSpec(memory_space=pltpu.HBM)
    vmem = pl.BlockSpec(memory_space=pltpu.VMEM)
    smem = pl.BlockSpec(memory_space=pltpu.SMEM)

    key_t, value_t = w_key.T, w_value.T
    prefix_rows = prefix_states.shape[0]
    near = prefix_states
    if 2 * prefix_rows != prefix_len:
        near = lax.all_gather(prefix_states, "cand", axis=0, tiled=True)
    height = size + head + 2 * share
    tail = prefix_rows * (cand_states.shape[1] // size) if near is prefix_states else prefix_len
    piece = pl.pallas_call(
        functools.partial(cut_kernel, (prefix_rows, prefix_len, cand_states.shape[1])),
        name="cut",
        out_shape=jax.ShapeDtypeStruct((height + tail, size), jnp.bfloat16),
        in_specs=[any_spec] * 5,
        out_specs=any_spec,
        scratch_shapes=[
            pltpu.VMEM((height + tail, size), jnp.bfloat16),
            pltpu.SemaphoreType.DMA((8,)),
            pltpu.SemaphoreType.DMA((8,)),
        ],
        compiler_params=pltpu.CompilerParams(vmem_limit_bytes=60 * 2**20),
    )(w_query, w_out, key_t, value_t, near)
    moved = along_line(piece, height)
    xs = [
        shift(k)(lax.dynamic_slice_in_dim(cand_states, (me + k) % n * rows, rows, 0))
        for k in range(1, n)
    ]
    across = other_core(piece)
    spreads = [spread(whole, v) for whole, v in moved]
    plan = tuple((masks, crossed) for _, masks, crossed in spreads[0])
    pieces = [v for s in spreads for v, _, _ in s]
    cos, sin = rotary_tables(prefix_len + cand_len, half, head)

    dims = (n, rows, cand_len, prefix_rows, prefix_len, depth, head, out_cols)
    count = len(spreads[0])
    every = rows + prefix_len
    early = pieces[: (n - 2) * count]
    last = pieces[(n - 2) * count :]
    normed, queries, pairs = pl.pallas_call(
        functools.partial(first_kernel, dims, nearest(n), plan),
        name="first",
        out_shape=[
            jax.ShapeDtypeStruct((depth // size, every, size), jnp.bfloat16),
            jax.ShapeDtypeStruct((n - 1, rows, head), jnp.bfloat16),
            jax.ShapeDtypeStruct((n - 1, every, 2 * share), jnp.bfloat16),
        ],
        in_specs=[hbm, vmem, vmem, vmem]
        + [vmem] * 4
        + [hbm] * 3
        + [vmem] * (len(xs) + len(early)),
        out_specs=[vmem] * 3,
        scratch_shapes=[
            pltpu.VMEM((rows, depth // n), jnp.bfloat16),
            pltpu.VMEM((depth, head), jnp.bfloat16),
            pltpu.VMEM((2 * share, depth), jnp.bfloat16),
            pltpu.VMEM((depth // size, prefix_len, size), jnp.bfloat16),
            pltpu.SemaphoreType.DMA((4,)),
        ],
        compiler_params=pltpu.CompilerParams(vmem_limit_bytes=24 * 2**20),
    )(
        cand_states, norm_gain.reshape(depth // size, 1, size), cos, sin,
        piece, across, last[0], last[count // 2],
        w_query, key_t, value_t, *xs, *early,
    )
    q_part, kv_part = pl.pallas_call(
        functools.partial(second_kernel, dims, nearest(n), plan),
        name="second",
        out_shape=[
            jax.ShapeDtypeStruct((rows, head), jnp.float32),
            jax.ShapeDtypeStruct((every, 2 * share), jnp.float32),
        ],
        in_specs=[vmem] * (1 + count - 2),
        out_specs=[vmem] * 2,
        compiler_params=pltpu.CompilerParams(vmem_limit_bytes=16 * 2**20),
    )(normed, *[v for i, v in enumerate(last) if i not in late(count)])
    return pl.pallas_call(
        functools.partial(last_kernel, dims, nearest(n), plan),
        name="main",
        out_shape=jax.ShapeDtypeStruct((rows, out_cols), jnp.bfloat16),
        in_specs=[vmem] * 5 + [smem, hbm] + [vmem] * (2 + len(pieces)),
        out_specs=hbm,
        scratch_shapes=[
            pltpu.VMEM((head, out_cols), jnp.bfloat16),
            pltpu.VMEM((n, every, 2 * share), jnp.bfloat16),
            pltpu.VMEM((n, rows, head), jnp.bfloat16),
            pltpu.VMEM((count, rows, size), jnp.bfloat16),
            pltpu.SemaphoreType.DMA,
            pltpu.SemaphoreType.DMA((count,)),
        ],
        compiler_params=pltpu.CompilerParams(vmem_limit_bytes=24 * 2**20),
    )(normed, queries, pairs, cos, sin, cand_lengths, w_out, q_part, kv_part, *pieces)


def solution(mesh):
    in_specs = (
        P(("query", "cand"), "tensor"),
        P(("query", "cand"), "tensor"),
        P(),
        P(None, "tensor"),
        P(None, "tensor"),
        P(None, "tensor"),
        P("tensor", None),
        P(("query", "cand")),
    )
    out_specs = P(("query", "cand", "tensor"), None)

    return jax.shard_map(body, mesh=mesh, in_specs=in_specs, out_specs=out_specs, check_vma=False)
```
